256 devices in a mesh: frame: 32 (over z, y_hi, core), head: 8 (over x, y_lo).
Axes of the slice: x: 4, y: 4 (y_hi: 2, y_lo: 2; y = y_hi * 2 + y_lo), z: 8, core: 2. Of those that a mesh axis runs over, the one named last changes fastest.
Arguments:
- queries: bfloat16 [32768, 3072], P(('frame', 'head')), may hold values from -64 to 64, as said below
- key_rows: bfloat16 [32768, 3072], P(('frame', 'head')), may hold values from -64 to 64, as said below
- value_rows: bfloat16 [32768, 3072], P(('frame', 'head')), may hold values from -24 to 24
- block_mask: int32 [256, 256], replicated, may hold values from 0 to 1, as said below
Outputs:
- attended: bfloat16 [32768, 3072], P(('frame', 'head'))
The draws below stay inside these ranges and needn't reach their ends.
Inputs may be any that keep to these rules, and one draw needn't show every extreme that they name: block_mask holds 0 or 1; every query block attends to all key blocks of its own frame; for two frames two or more apart, the query blocks of one attend to exactly one key block of the other (the same one for all of them), and some query blocks may attend to none of it. queries are finite reals. `key_rows`: keys are finite reals.
All inputs are finite; a program needn't handle non-finite values.
Results may differ from the reference program's by a relative error of at most 0.0037.
Values may be sent and summed in bfloat16 or wider, within the bound.
No kernel may reach another device: no remote copies, remote signals or barrier semaphores. Data moves between devices by JAX's collectives and lax.ppermute only.
A program may use at most 128 MiB of HBM per device.

```python
import math
import jax
import jax.numpy as jnp
from jax import lax

HEADS = 24
HDIM = 128
BLOCK = 128
BF = 8
FT = 1024
FRAMES = 32
TOKENS = 32768
NBLK = 256
WIDTH = 3072


def query_key_pair(key):
    width_all = HEADS * HDIM
    base_query = jnp.clip(jax.random.normal(jax.random.fold_in(key, 11), (TOKENS, width_all), jnp.float32) * 1.4, -8.0, 8.0)
    base_key = jnp.clip(jax.random.normal(jax.random.fold_in(key, 12), (TOKENS, width_all), jnp.float32) * 1.4, -8.0, 8.0)
    return (base_query, base_key)


def draw_queries(key, part):
    return query_key_pair(key)[0].astype(jnp.bfloat16)


def draw_key_rows(key, part):
    return query_key_pair(key)[1].astype(jnp.bfloat16)


def draw_block_mask(key, part):
    radius = jax.random.randint(jax.random.fold_in(key, 21), (FRAMES, FRAMES), 1, 4)
    anchor_table = jax.random.randint(jax.random.fold_in(key, 22), (FRAMES, FRAMES), 0, BF)
    block_index = jnp.arange(NBLK, dtype=jnp.int32)
    frame_of = block_index // BF
    place_of = block_index % BF
    distance = jnp.abs(frame_of[:, None] - frame_of[None, :])
    pair_radius = radius[frame_of[:, None], frame_of[None, :]]
    anchor = anchor_table[frame_of[:, None], frame_of[None, :]]
    block_gap = jnp.abs(place_of[:, None] - place_of[None, :])
    reach = jnp.where(distance < 4, 2, jnp.where(distance < 8, 1, 0))
    far_active = (place_of[None, :] == anchor) & (jnp.abs(place_of[:, None] - anchor) <= reach)
    active = jnp.where(distance == 0, True, jnp.where(distance == 1, block_gap <= pair_radius, far_active))
    return active.astype(jnp.int32)


def level_of(key, dims, shards, least, largest):
    level = 1.0
    for position, parts in shards:
        steps = jax.random.uniform(jax.random.fold_in(jax.random.fold_in(key, 6), position), (parts,), jnp.float32, least / len(shards), largest / len(shards))
        level = level * jnp.repeat(jnp.exp(steps), dims[position] // parts).reshape((-1,) + (1,) * (len(dims) - 1 - position))
    return level


def scatter_about(stream_key, shape, width, most, split=(), held_as=jnp.bfloat16):
    drawn = jax.random.normal(stream_key, shape, jnp.float32) * width
    if len(split) > 0:
        drawn = level_of(stream_key, shape, split, -0.22, 0.18) * drawn
    return jnp.clip(drawn, min=-most, max=most).astype(held_as)


def setup_inputs(seed: int = 0) -> dict:
    splits = jax.random.split(jax.random.key(seed), 5)
    queries = draw_queries(jax.random.fold_in(splits[4], 71), 0)
    key_rows = draw_key_rows(jax.random.fold_in(splits[4], 71), 0)
    value_rows = scatter_about(splits[2], (TOKENS, WIDTH), 4.0, 24.0, ((0, 256),))
    block_mask = draw_block_mask(jax.random.fold_in(splits[4], 71), 0)
    return dict(queries=queries, key_rows=key_rows, value_rows=value_rows, block_mask=block_mask)


def reference(queries, key_rows, value_rows, block_mask):
    row_width = HEADS * HDIM
    score_scale = 1.0 / math.sqrt(HDIM)
    mask_grid = block_mask.reshape(FRAMES, BF, FRAMES, BF)
    used_blocks = lax.optimization_barrier(jnp.max(mask_grid, axis=1))
    block_ids = jnp.arange(BF, dtype=jnp.int32)
    chosen = jnp.minimum(lax.optimization_barrier(jnp.sum(used_blocks * block_ids[None, None, :], axis=-1)), BF - 1).astype(jnp.int32)
    query_frames = queries.reshape(FRAMES, FT, row_width)
    zero_frame = jnp.zeros((1, FT, row_width), jnp.bfloat16)
    key_pad = jnp.concatenate([zero_frame, key_rows.reshape(FRAMES, FT, row_width), zero_frame], axis=0)
    value_pad = jnp.concatenate([zero_frame, value_rows.reshape(FRAMES, FT, row_width), zero_frame], axis=0)
    key_blocks = key_rows.reshape(FRAMES, BF, BLOCK, row_width)
    value_blocks = value_rows.reshape(FRAMES, BF, BLOCK, row_width)
    mask_pad = jnp.pad(mask_grid, ((0, 0), (0, 0), (1, 1), (0, 0)))
    frame_ids = jnp.arange(FRAMES, dtype=jnp.int32)

    def one_frame(frame_id):
        near_keys = lax.dynamic_slice_in_dim(key_pad, frame_id, 3, 0).reshape(3 * FT, row_width)
        near_values = lax.dynamic_slice_in_dim(value_pad, frame_id, 3, 0).reshape(3 * FT, row_width)
        picked = lax.dynamic_index_in_dim(chosen, frame_id, 0, keepdims=False)
        far_keys = key_blocks[frame_ids, picked].reshape(FRAMES * BLOCK, row_width)
        far_values = value_blocks[frame_ids, picked].reshape(FRAMES * BLOCK, row_width)
        frame_rows = lax.dynamic_index_in_dim(mask_pad, frame_id, 0, keepdims=False)
        near_mask = lax.dynamic_slice_in_dim(frame_rows, frame_id, 3, 1).reshape(BF, 3 * BF)
        own_rows = frame_rows[:, 1:-1, :]
        match = (block_ids[None, None, :] == picked[None, :, None]).astype(jnp.int32)
        far_mask = lax.optimization_barrier(jnp.sum(own_rows * match, axis=2))
        distant = (jnp.abs(frame_ids - frame_id) >= 2).astype(jnp.int32)
        far_mask = far_mask * distant[None, :]
        block_on = jnp.concatenate([near_mask, far_mask], axis=1) > 0
        token_on = jnp.repeat(jnp.repeat(block_on, BLOCK, axis=0), BLOCK, axis=1)
        all_keys = jnp.concatenate([near_keys, far_keys], axis=0)
        all_values = jnp.concatenate([near_values, far_values], axis=0)
        frame_query = lax.dynamic_index_in_dim(query_frames, frame_id, 0, keepdims=False)

        def one_head(head_no):
            head_query = lax.dynamic_slice_in_dim(frame_query, head_no * HDIM, HDIM, 1)
            head_keys = lax.dynamic_slice_in_dim(all_keys, head_no * HDIM, HDIM, 1)
            head_values = lax.dynamic_slice_in_dim(all_values, head_no * HDIM, HDIM, 1)
            scores = lax.dot_general(head_query, head_keys, (((1,), (1,)), ((), ())), preferred_element_type=jnp.float32) * score_scale
            scores = jnp.where(token_on, scores, -1e+30)
            row_top = lax.optimization_barrier(jnp.max(scores, axis=1, keepdims=True))
            weights = jnp.exp(scores - row_top)
            denominator = lax.optimization_barrier(jnp.sum(weights, axis=1, keepdims=True))
            result = jnp.dot(weights.astype(jnp.bfloat16), head_values, preferred_element_type=jnp.float32) / denominator
            return result.astype(jnp.bfloat16)
        heads = lax.map(one_head, jnp.arange(HEADS, dtype=jnp.int32))
        return jnp.transpose(heads, (1, 0, 2)).reshape(FT, row_width)
    results = lax.map(one_frame, frame_ids)
    return results.reshape(TOKENS, row_width)
```

```python
import functools
import math

import jax
import jax.numpy as jnp
from jax import lax
from jax.experimental import pallas as pl
from jax.experimental.pallas import tpu as pltpu
from jax.sharding import PartitionSpec as P

HDIM = 128
BLOCK = 128
BF = 8
FT = BF * BLOCK
HEADS_LOCAL = 3
GROUP = 4
NEG = -1e30
SCALE2 = math.log2(math.e) / math.sqrt(HDIM)
NT = (((1,), (1,)), ((), ()))
NN = (((1,), (0,)), ((), ()))


def dot(a, b, dims):
    return lax.dot_general(a, b, dims, preferred_element_type=jnp.float32)


def pack_kernel(q_ref, k_ref, v_ref, out_ref):
    heads = q_ref.shape[1] // HDIM
    for h in range(heads):
        cols = slice(h * HDIM, (h + 1) * HDIM)
        base = 2 * h * HDIM
        out_ref[0, :, base : base + HDIM] = k_ref[:, cols]
        out_ref[0, :, base + HDIM : base + 2 * HDIM] = v_ref[:, cols]
    out_ref[0, :, 2 * heads * HDIM :] = q_ref[...]


def pack(queries, keys, values, peers):
    rows, width = queries.shape
    local = width // peers
    spec = pl.BlockSpec((rows, local), lambda j: (0, j))
    return pl.pallas_call(
        pack_kernel,
        grid=(peers,),
        in_specs=[spec] * 3,
        out_specs=pl.BlockSpec((1, rows, 3 * local), lambda j: (j, 0, 0)),
        out_shape=jax.ShapeDtypeStruct((peers, rows, 3 * local), queries.dtype),
        name="pack",
    )(queries, keys, values)


def unpack_kernel(part_ref, out_ref):
    out_ref[...] = part_ref[0]


def unpack(parts):
    peers, rows, local = parts.shape
    return pl.pallas_call(
        unpack_kernel,
        grid=(peers,),
        in_specs=[pl.BlockSpec((1, rows, local), lambda j: (j, 0, 0))],
        out_specs=pl.BlockSpec((rows, local), lambda j: (0, j)),
        out_shape=jax.ShapeDtypeStruct((rows, peers * local), parts.dtype),
        name="unpack",
    )(parts)


def select_kernel(pick_ref, kv_ref, out_ref):
    base = pl.program_id(0) * out_ref.shape[0]
    for i in range(out_ref.shape[0]):
        out_ref[i] = kv_ref[pick_ref[base + i]]


def select_blocks(picks, blocks, head):
    frames = picks.shape[0]
    step = 8
    count, rows, _ = blocks.shape
    width = 2 * HDIM
    return pl.pallas_call(
        select_kernel,
        grid_spec=pltpu.PrefetchScalarGridSpec(
            num_scalar_prefetch=1,
            grid=(frames // step,),
            in_specs=[pl.BlockSpec((count, rows, width), lambda i, p: (0, 0, head))],
            out_specs=pl.BlockSpec((step, rows, width), lambda i, p: (i, 0, 0)),
        ),
        out_shape=jax.ShapeDtypeStruct((frames, rows, width), blocks.dtype),
        name="select",
    )(picks, blocks)


def near_kernel(on_ref, q_ref, own_ref, before_ref, after_ref, o_ref, ml_ref):
    tile = q_ref.shape[0]
    sub = tile // BLOCK
    first = pl.program_id(0) * sub
    query = q_ref[...]
    parts = [dot(query, own_ref[:, :HDIM], NT)]
    for side, ref in enumerate((before_ref, after_ref)):
        scores = dot(query, ref[:, :HDIM], NT)
        rows = []
        for s in range(sub):
            cols = []
            for b in range(BF):
                bias = jnp.where(on_ref[first + s, side * BF + b] > 0, 0.0, NEG)
                cols.append(
                    scores[s * BLOCK : (s + 1) * BLOCK, b * BLOCK : (b + 1) * BLOCK] + bias
                )
            rows.append(jnp.concatenate(cols, axis=1))
        parts.append(jnp.concatenate(rows, axis=0))
    top = functools.reduce(jnp.maximum, [jnp.max(p, axis=1, keepdims=True) for p in parts])
    total = jnp.zeros((tile, 1), jnp.float32)
    summed = jnp.zeros((tile, HDIM), jnp.float32)
    for part, ref in zip(parts, (own_ref, before_ref, after_ref)):
        weights = jnp.exp2((part - top) * SCALE2)
        total = total + jnp.sum(weights, axis=1, keepdims=True)
        summed = summed + dot(weights.astype(jnp.bfloat16), ref[:, HDIM:], NN)
    o_ref[...] = summed
    half = ml_ref.shape[1] // 2
    ml_ref[:, :half] = jnp.broadcast_to(top, (tile, half))
    ml_ref[:, half:] = jnp.broadcast_to(total, (tile, half))


def near_attention(near_on, mixed, head, before, after):
    tile = 256
    rows, width = mixed.shape
    column = width // HDIM - HEADS_LOCAL + head
    whole = pl.BlockSpec((rows, 2 * HDIM), lambda i, on: (0, head))
    flops = 4 * rows * 3 * rows * HDIM
    return pl.pallas_call(
        near_kernel,
        grid_spec=pltpu.PrefetchScalarGridSpec(
            num_scalar_prefetch=1,
            grid=(rows // tile,),
            in_specs=[pl.BlockSpec((tile, HDIM), lambda i, on: (i, column)), whole, whole, whole],
            out_specs=[pl.BlockSpec((tile, HDIM), lambda i, on: (i, 0))] * 2,
        ),
        out_shape=[jax.ShapeDtypeStruct((rows, HDIM), jnp.float32)] * 2,
        cost_estimate=pl.CostEstimate(
            flops=flops, bytes_accessed=4 * rows * 2 * HDIM * 2, transcendentals=3 * rows * rows
        ),
        name="near",
    )(near_on, mixed, mixed, before, after)


def far_kernel(list_ref, count_ref, q_ref, kv_ref, o_ref, ml_ref, out_ref, m_s, l_s, acc_s):
    half = ml_ref.shape[1] // 2
    m_s[...] = ml_ref[:, :1]
    l_s[...] = ml_ref[:, half : half + 1]
    acc_s[...] = o_ref[...]
    blocks = q_ref.shape[0] // BLOCK
    most = count_ref[0]
    for qb in range(1, blocks):
        most = jnp.maximum(most, count_ref[qb])

    def step(t, carry):
        for qb in range(blocks):
            rows = slice(qb * BLOCK, (qb + 1) * BLOCK)
            query = q_ref[rows, :]
            frames = [list_ref[qb, t * GROUP + i] for i in range(GROUP)]
            scores = []
            for i in range(GROUP):
                bias = jnp.where(t * GROUP + i < count_ref[qb], 0.0, NEG)
                scores.append(dot(query, kv_ref[frames[i], :, :HDIM], NT) + bias)
            old = m_s[rows, :]
            peak = functools.reduce(jnp.maximum, scores)
            top = jnp.maximum(old, jnp.max(peak, axis=1, keepdims=True))
            fade = jnp.exp2((old - top) * SCALE2)
            acc = acc_s[rows, :] * fade
            mass = jnp.zeros((BLOCK, BLOCK), jnp.float32)
            for i in range(GROUP):
                weights = jnp.exp2((scores[i] - top) * SCALE2)
                mass = mass + weights
                acc = acc + dot(weights.astype(jnp.bfloat16), kv_ref[frames[i], :, HDIM:], NN)
            m_s[rows, :] = top
            l_s[rows, :] = l_s[rows, :] * fade + jnp.sum(mass, axis=1, keepdims=True)
            acc_s[rows, :] = acc
        return carry

    lax.fori_loop(0, (most + GROUP - 1) // GROUP, step, 0)
    out_ref[...] = (acc_s[...] / l_s[...]).astype(out_ref.dtype)


def far_attention(order, counts, mixed, head, far, near_o, near_ml):
    rows, width = mixed.shape
    column = width // HDIM - HEADS_LOCAL + head
    frames = far.shape[0]
    full = pl.BlockSpec((rows, HDIM), lambda i, a, b: (0, 0))
    return pl.pallas_call(
        far_kernel,
        grid_spec=pltpu.PrefetchScalarGridSpec(
            num_scalar_prefetch=2,
            grid=(1,),
            in_specs=[
                pl.BlockSpec((rows, HDIM), lambda i, a, b: (0, column)),
                pl.BlockSpec((frames, BLOCK, 2 * HDIM), lambda i, a, b: (0, 0, 0)),
                full,
                full,
            ],
            out_specs=full,
            scratch_shapes=[
                pltpu.VMEM((rows, 1), jnp.float32),
                pltpu.VMEM((rows, 1), jnp.float32),
                pltpu.VMEM((rows, HDIM), jnp.float32),
            ],
        ),
        out_shape=jax.ShapeDtypeStruct((rows, HDIM), mixed.dtype),
        cost_estimate=pl.CostEstimate(
            flops=rows * frames * BLOCK * HDIM,
            bytes_accessed=frames * BLOCK * 2 * HDIM * 2,
            transcendentals=rows * frames * BLOCK // 4,
        ),
        name="far",
    )(order, counts, mixed, far, near_o, near_ml)


def mask_tables(block_mask, frame_id, frame_count):
    block_ids = jnp.arange(BF, dtype=jnp.int32)
    frame_ids = jnp.arange(frame_count, dtype=jnp.int32)
    towards = lax.dynamic_slice_in_dim(block_mask, frame_id * BF, BF, 1)
    towards = jnp.max(towards.reshape(frame_count, BF, BF), axis=1)
    outgoing = jnp.minimum(jnp.sum(towards * block_ids[None, :], axis=1), BF - 1)
    own = lax.dynamic_slice_in_dim(block_mask, frame_id * BF, BF, 0)
    padded = jnp.pad(own, ((0, 0), (BF, BF)))
    beside = lax.dynamic_slice_in_dim(padded, frame_id * BF, 3 * BF, 1)
    near_on = jnp.concatenate([beside[:, :BF], beside[:, 2 * BF :]], axis=1)
    distant = (jnp.abs(frame_ids - frame_id) >= 2).astype(jnp.int32)
    active = jnp.max(own.reshape(BF, frame_count, BF), axis=2) * distant[None, :]
    upto = (frame_ids[:, None] <= frame_ids[None, :]).astype(jnp.int32)
    place = jnp.sum(active[:, :, None] * upto[None, :, :], axis=1)
    counts = jnp.sum(active, axis=1)
    slots = jnp.where(active > 0, place - 1, -1)
    hit = (slots[:, :, None] == frame_ids[None, None, :]).astype(jnp.int32)
    order = jnp.sum(hit * frame_ids[None, :, None], axis=1)
    return outgoing, near_on, order, counts


def body(queries, key_rows, value_rows, block_mask):
    frame_count = lax.axis_size("frame")
    peers = lax.axis_size("head")
    frame_id = lax.axis_index("frame")
    exchange = functools.partial(lax.all_to_all, split_axis=0, concat_axis=0, tiled=True)
    up = [(i, i + 1) for i in range(frame_count - 1)]
    down = [(j, i) for i, j in up]
    heads = range(HEADS_LOCAL)
    outgoing, near_on, order, counts = mask_tables(block_mask, frame_id, frame_count)
    packed = pack(queries, key_rows, value_rows, peers)
    blocks = exchange(packed, "head")
    mixed = blocks.reshape(FT, blocks.shape[2])
    far = []
    for head in heads:
        parcel = select_blocks(outgoing, blocks, head)
        far.append(exchange(parcel, "frame"))
    pairs = mixed[:, : 2 * HDIM * HEADS_LOCAL]
    before = lax.ppermute(pairs, "frame", up)
    after = lax.ppermute(pairs, "frame", down)
    outs = []
    for head in heads:
        near_o, near_ml = near_attention(near_on, mixed, head, before, after)
        outs.append(far_attention(order, counts, mixed, head, far[head], near_o, near_ml))
    result = jnp.concatenate(outs, axis=1).reshape(peers, BLOCK, HEADS_LOCAL * HDIM)
    return unpack(exchange(result, "head"))


def solution(mesh):
    placed = (
        P(("frame", "head"), None),
        P(("frame", "head"), None),
        P(("frame", "head"), None),
        P(),
    )
    return jax.shard_map(
        body, mesh=mesh, in_specs=placed, out_specs=P(("frame", "head"), None), check_vma=False
    )
```

```python
import functools
import math

import jax
import jax.numpy as jnp
from jax import lax
from jax.experimental import pallas as pl
from jax.experimental.pallas import tpu as pltpu
from jax.sharding import PartitionSpec as P

HDIM = 128
BLOCK = 128
BF = 8
FT = BF * BLOCK
HEADS_LOCAL = 3
GROUP = 2
PACK_STEPS = 4
SELECT_STEPS = 2
PARAMS = pltpu.CompilerParams(vmem_limit_bytes=24 << 20)
NEG = -1e30
SCALE2 = math.log2(math.e) / math.sqrt(HDIM)
NT = (((1,), (1,)), ((), ()))
NN = (((1,), (0,)), ((), ()))


def in_hbm(*arrays):
    return [pltpu.with_memory_space_constraint(a, pltpu.HBM) for a in arrays]


def dot(a, b, dims):
    return lax.dot_general(a, b, dims, preferred_element_type=jnp.float32)


def pack_kernel(q_ref, k_ref, v_ref, out_ref):
    peers = out_ref.shape[0]
    local = q_ref.shape[1] // peers
    for j in range(peers):
        for h in range(local // HDIM):
            cols = slice(j * local + h * HDIM, j * local + (h + 1) * HDIM)
            base = 2 * h * HDIM
            out_ref[j, :, base : base + HDIM] = k_ref[:, cols]
            out_ref[j, :, base + HDIM : base + 2 * HDIM] = v_ref[:, cols]
        out_ref[j, :, 2 * local :] = q_ref[:, j * local : (j + 1) * local]


def pack(queries, keys, values, peers):
    rows, width = queries.shape
    local = width // peers
    tile = rows // PACK_STEPS
    spec = pl.BlockSpec((tile, width), lambda i: (i, 0))
    return pl.pallas_call(
        pack_kernel,
        grid=(PACK_STEPS,),
        in_specs=[spec] * 3,
        out_specs=pl.BlockSpec((peers, tile, 3 * local), lambda i: (0, i, 0)),
        out_shape=pltpu.HBM((peers, rows, 3 * local), queries.dtype),
        compiler_params=PARAMS,
        name="pack",
    )(*in_hbm(queries, keys, values))


def unpack_kernel(part_ref, out_ref):
    peers, _, local = part_ref.shape
    for j in range(peers):
        out_ref[:, j * local : (j + 1) * local] = part_ref[j]


def unpack(parts):
    peers, rows, local = parts.shape
    tile = rows // PACK_STEPS
    return pl.pallas_call(
        unpack_kernel,
        grid=(PACK_STEPS,),
        in_specs=[pl.BlockSpec((peers, tile, local), lambda i: (0, i, 0))],
        out_specs=pl.BlockSpec((tile, peers * local), lambda i: (i, 0)),
        out_shape=jax.ShapeDtypeStruct((rows, peers * local), parts.dtype),
        compiler_params=PARAMS,
        name="unpack",
    )(parts)


def select_kernel(pick_ref, kv_ref, out_ref):
    base = pl.program_id(0) * out_ref.shape[0]
    for i in range(out_ref.shape[0]):
        out_ref[i] = kv_ref[pick_ref[base + i]]


def select_blocks(picks, blocks, head):
    frames = picks.shape[0]
    step = frames // SELECT_STEPS
    count, rows, _ = blocks.shape
    width = 2 * HDIM
    return pl.pallas_call(
        select_kernel,
        grid_spec=pltpu.PrefetchScalarGridSpec(
            num_scalar_prefetch=1,
            grid=(frames // step,),
            in_specs=[pl.BlockSpec((count, rows, width), lambda i, p: (0, 0, head))],
            out_specs=pl.BlockSpec((step, rows, width), lambda i, p: (i, 0, 0)),
        ),
        out_shape=pltpu.HBM((frames, rows, width), blocks.dtype),
        compiler_params=PARAMS,
        name="select",
    )(picks, blocks)


def near_kernel(on_ref, q_ref, own_ref, before_ref, after_ref, o_ref, m_ref, l_ref):
    tile = q_ref.shape[0]
    sub = tile // BLOCK
    first = pl.program_id(0) * sub
    query = q_ref[...]
    parts = [dot(query, own_ref[:, :HDIM], NT)]
    for side, ref in enumerate((before_ref, after_ref)):
        scores = dot(query, ref[:, :HDIM], NT)
        rows = []
        for s in range(sub):
            cols = []
            for b in range(BF):
                bias = jnp.where(on_ref[first + s, side * BF + b] > 0, 0.0, NEG)
                cols.append(
                    scores[s * BLOCK : (s + 1) * BLOCK, b * BLOCK : (b + 1) * BLOCK] + bias
                )
            rows.append(jnp.concatenate(cols, axis=1))
        parts.append(jnp.concatenate(rows, axis=0))
    top = functools.reduce(jnp.maximum, [jnp.max(p, axis=1, keepdims=True) for p in parts])
    mass = jnp.zeros((tile, HDIM), jnp.float32)
    summed = jnp.zeros((tile, HDIM), jnp.float32)
    for part, ref in zip(parts, (own_ref, before_ref, after_ref)):
        weights = jnp.exp2((part - top) * SCALE2)
        for b in range(BF):
            mass = mass + weights[:, b * BLOCK : (b + 1) * BLOCK]
        summed = summed + dot(weights.astype(jnp.bfloat16), ref[:, HDIM:], NN)
    o_ref[...] = summed
    m_ref[...] = jnp.broadcast_to(top, (tile, HDIM))
    l_ref[...] = mass


def near_attention(near_on, mixed, head, before, after):
    tile = 256
    rows, width = mixed.shape
    column = width // HDIM - HEADS_LOCAL + head
    whole = pl.BlockSpec((rows, 2 * HDIM), lambda i, on: (0, head))
    flops = 4 * rows * 3 * rows * HDIM
    return pl.pallas_call(
        near_kernel,
        grid_spec=pltpu.PrefetchScalarGridSpec(
            num_scalar_prefetch=1,
            grid=(rows // tile,),
            in_specs=[pl.BlockSpec((tile, HDIM), lambda i, on: (i, column)), whole, whole, whole],
            out_specs=[pl.BlockSpec((tile, HDIM), lambda i, on: (i, 0))] * 3,
        ),
        out_shape=[pltpu.HBM((rows, HDIM), jnp.float32)] * 3,
        cost_estimate=pl.CostEstimate(
            flops=flops, bytes_accessed=4 * rows * 2 * HDIM * 2, transcendentals=3 * rows * rows
        ),
        compiler_params=PARAMS,
        name="near",
    )(near_on, mixed, mixed, before, after)


def far_kernel(list_ref, count_ref, q_ref, kv_ref, o_ref, m_ref, l_ref, out_ref, m_s, l_s, acc_s):
    m_s[...] = m_ref[...]
    l_s[...] = l_ref[...]
    acc_s[...] = o_ref[...]
    blocks = q_ref.shape[0] // BLOCK
    most = count_ref[0]
    for qb in range(1, blocks):
        most = jnp.maximum(most, count_ref[qb])

    def step(t, carry):
        for qb in range(blocks):
            rows = slice(qb * BLOCK, (qb + 1) * BLOCK)
            query = q_ref[rows, :]
            frames = [list_ref[qb, t * GROUP + i] for i in range(GROUP)]
            keys = jnp.concatenate([kv_ref[f, :, :HDIM] for f in frames], axis=0)
            values = jnp.concatenate([kv_ref[f, :, HDIM:] for f in frames], axis=0)
            raw = dot(query, keys, NT)
            scores = []
            for i in range(GROUP):
                bias = jnp.where(t * GROUP + i < count_ref[qb], 0.0, NEG)
                scores.append(raw[:, i * BLOCK : (i + 1) * BLOCK] + bias)
            old = m_s[rows, :]
            peak = functools.reduce(jnp.maximum, scores)
            top = jnp.maximum(old, jnp.max(peak, axis=1, keepdims=True))
            fade = jnp.exp2((old - top) * SCALE2)
            weights = [jnp.exp2((s - top) * SCALE2) for s in scores]
            rounded = jnp.concatenate([w.astype(jnp.bfloat16) for w in weights], axis=1)
            m_s[rows, :] = top
            l_s[rows, :] = l_s[rows, :] * fade + functools.reduce(jnp.add, weights)
            acc_s[rows, :] = acc_s[rows, :] * fade + dot(rounded, values, NN)
        return carry

    lax.fori_loop(0, (most + GROUP - 1) // GROUP, step, 0)
    total = jnp.sum(l_s[...], axis=1, keepdims=True)
    out_ref[...] = (acc_s[...] / total).astype(out_ref.dtype)


def far_attention(order, counts, mixed, head, far, near):
    rows, width = mixed.shape
    column = width // HDIM - HEADS_LOCAL + head
    frames = far.shape[0]
    full = pl.BlockSpec((rows, HDIM), lambda i, a, b: (0, 0))
    return pl.pallas_call(
        far_kernel,
        grid_spec=pltpu.PrefetchScalarGridSpec(
            num_scalar_prefetch=2,
            grid=(1,),
            in_specs=[
                pl.BlockSpec((rows, HDIM), lambda i, a, b: (0, column)),
                pl.BlockSpec((frames, BLOCK, 2 * HDIM), lambda i, a, b: (0, 0, 0)),
                full,
                full,
                full,
            ],
            out_specs=full,
            scratch_shapes=[
                pltpu.VMEM((rows, HDIM), jnp.float32),
                pltpu.VMEM((rows, HDIM), jnp.float32),
                pltpu.VMEM((rows, HDIM), jnp.float32),
            ],
        ),
        out_shape=jax.ShapeDtypeStruct((rows, HDIM), mixed.dtype),
        cost_estimate=pl.CostEstimate(
            flops=rows * frames * BLOCK * HDIM,
            bytes_accessed=frames * BLOCK * 2 * HDIM * 2,
            transcendentals=rows * frames * BLOCK // 4,
        ),
        compiler_params=PARAMS,
        name="far",
    )(order, counts, mixed, far, *in_hbm(*near))


def mask_tables(block_mask, frame_id, frame_count):
    block_ids = jnp.arange(BF, dtype=jnp.int32)
    frame_ids = jnp.arange(frame_count, dtype=jnp.int32)
    towards = lax.dynamic_slice_in_dim(block_mask, frame_id * BF, BF, 1)
    towards = jnp.max(towards.reshape(frame_count, BF, BF), axis=1)
    outgoing = jnp.minimum(jnp.sum(towards * block_ids[None, :], axis=1), BF - 1)
    own = lax.dynamic_slice_in_dim(block_mask, frame_id * BF, BF, 0)
    padded = jnp.pad(own, ((0, 0), (BF, BF)))
    beside = lax.dynamic_slice_in_dim(padded, frame_id * BF, 3 * BF, 1)
    near_on = jnp.concatenate([beside[:, :BF], beside[:, 2 * BF :]], axis=1)
    distant = (jnp.abs(frame_ids - frame_id) >= 2).astype(jnp.int32)
    active = jnp.max(own.reshape(BF, frame_count, BF), axis=2) * distant[None, :]
    upto = (frame_ids[:, None] <= frame_ids[None, :]).astype(jnp.int32)
    place = jnp.sum(active[:, :, None] * upto[None, :, :], axis=1)
    counts = jnp.sum(active, axis=1)
    slots = jnp.where(active > 0, place - 1, -1)
    hit = (slots[:, :, None] == frame_ids[None, None, :]).astype(jnp.int32)
    order = jnp.sum(hit * frame_ids[None, :, None], axis=1)
    return outgoing, near_on, order, counts


def body(queries, key_rows, value_rows, block_mask):
    frame_count = lax.axis_size("frame")
    peers = lax.axis_size("head")
    frame_id = lax.axis_index("frame")
    exchange = functools.partial(lax.all_to_all, split_axis=0, concat_axis=0, tiled=True)
    up = [(i, i + 1) for i in range(frame_count - 1)]
    down = [(j, i) for i, j in up]
    heads = range(HEADS_LOCAL)
    outgoing, near_on, order, counts = mask_tables(block_mask, frame_id, frame_count)
    packed = pack(queries, key_rows, value_rows, peers)
    blocks = exchange(packed, "head")
    mixed = blocks.reshape(FT, blocks.shape[2])
    far = []
    for head in heads:
        parcel = select_blocks(outgoing, blocks, head)
        far.append(exchange(parcel, "frame"))
    pairs = mixed[:, : 2 * HDIM * HEADS_LOCAL]
    before = lax.ppermute(pairs, "frame", up)
    after = lax.ppermute(pairs, "frame", down)
    outs = []
    for head in heads:
        near = near_attention(near_on, mixed, head, before, after)
        outs.append(far_attention(order, counts, mixed, head, far[head], near))
    result = jnp.concatenate(outs, axis=1).reshape(peers, BLOCK, HEADS_LOCAL * HDIM)
    return unpack(exchange(result, "head"))


def solution(mesh):
    placed = (
        P(("frame", "head"), None),
        P(("frame", "head"), None),
        P(("frame", "head"), None),
        P(),
    )
    return jax.shard_map(
        body, mesh=mesh, in_specs=placed, out_specs=P(("frame", "head"), None), check_vma=False
    )
```

```python
import functools
import math

import jax
import jax.numpy as jnp
from jax import lax
from jax.experimental import pallas as pl
from jax.experimental.pallas import tpu as pltpu
from jax.sharding import PartitionSpec as P

HDIM = 128
BLOCK = 128
BF = 8
FT = BF * BLOCK
HEADS_LOCAL = 3
GROUP = 2
PACK_STEPS = 4
SELECT_STEPS = 2
PARAMS = pltpu.CompilerParams(vmem_limit_bytes=24 << 20)
NEG = -1e30
SCALE2 = math.log2(math.e) / math.sqrt(HDIM)
NT = (((1,), (1,)), ((), ()))
NN = (((1,), (0,)), ((), ()))


def in_hbm(*arrays):
    return [pltpu.with_memory_space_constraint(a, pltpu.HBM) for a in arrays]


def dot(a, b, dims):
    return lax.dot_general(a, b, dims, preferred_element_type=jnp.float32)


def lead_kernel(k_ref, v_ref, out_ref):
    peers = out_ref.shape[0]
    local = k_ref.shape[1] // peers
    for j in range(peers):
        out_ref[j, :, :HDIM] = k_ref[:, j * local : j * local + HDIM]
        out_ref[j, :, HDIM:] = v_ref[:, j * local : j * local + HDIM]


def pack_lead(keys, values, peers):
    rows, width = keys.shape
    tile = rows // PACK_STEPS
    spec = pl.BlockSpec((tile, width), lambda i: (i, 0))
    return pl.pallas_call(
        lead_kernel,
        grid=(PACK_STEPS,),
        in_specs=[spec] * 2,
        out_specs=pl.BlockSpec((peers, tile, 2 * HDIM), lambda i: (0, i, 0)),
        out_shape=pltpu.HBM((peers, rows, 2 * HDIM), keys.dtype),
        compiler_params=PARAMS,
        name="lead",
    )(*in_hbm(keys, values))


def rest_kernel(me_ref, q_ref, k_ref, v_ref, *out_refs):
    peers = len(out_refs)
    local = q_ref.shape[1] // peers
    heads = local // HDIM
    for d, out_ref in enumerate(out_refs):
        base = lax.rem(me_ref[0] + d, peers) * local
        for h in range(1, heads):
            cols = pl.ds(pl.multiple_of(base + h * HDIM, HDIM), HDIM)
            left = 2 * (h - 1) * HDIM
            out_ref[:, left : left + HDIM] = k_ref[:, cols]
            out_ref[:, left + HDIM : left + 2 * HDIM] = v_ref[:, cols]
        left = 2 * (heads - 1) * HDIM
        for h in range(heads):
            cols = pl.ds(pl.multiple_of(base + h * HDIM, HDIM), HDIM)
            out_ref[:, left + h * HDIM : left + (h + 1) * HDIM] = q_ref[:, cols]


def pack_rest(me, queries, keys, values, peers):
    rows, width = queries.shape
    local = width // peers
    size = 3 * local - 2 * HDIM
    tile = rows // PACK_STEPS
    spec = pl.BlockSpec((tile, width), lambda i, m: (i, 0))
    return pl.pallas_call(
        rest_kernel,
        grid_spec=pltpu.PrefetchScalarGridSpec(
            num_scalar_prefetch=1,
            grid=(PACK_STEPS,),
            in_specs=[spec] * 3,
            out_specs=[pl.BlockSpec((tile, size), lambda i, m: (i, 0))] * peers,
        ),
        out_shape=[pltpu.HBM((rows, size), queries.dtype)] * peers,
        compiler_params=PARAMS,
        name="rest",
    )(me, *in_hbm(queries, keys, values))


def gather_kernel(me_ref, lead_ref, *refs):
    parts, (mixed_ref, pairs_ref) = refs[:-2], refs[-2:]
    peers = len(parts)
    split = pairs_ref.shape[2] - 2 * HDIM
    mixed_ref[:, :, : 2 * HDIM] = lead_ref[...]
    pairs_ref[:, :, : 2 * HDIM] = lead_ref[...]
    for d, ref in enumerate(parts):
        block = lax.rem(me_ref[0] - d + peers, peers)
        part = ref[...]
        mixed_ref[block, :, 2 * HDIM :] = part
        pairs_ref[block, :, 2 * HDIM :] = part[:, :split]


def assemble(me, lead, parts):
    peers, rows, _ = lead.shape
    size = parts[0].shape[1]
    local = (size + 2 * HDIM) // 3
    tile = rows // PACK_STEPS
    return pl.pallas_call(
        gather_kernel,
        grid_spec=pltpu.PrefetchScalarGridSpec(
            num_scalar_prefetch=1,
            grid=(PACK_STEPS,),
            in_specs=[pl.BlockSpec((peers, tile, 2 * HDIM), lambda i, m: (0, i, 0))]
            + [pl.BlockSpec((tile, size), lambda i, m: (i, 0))] * peers,
            out_specs=[
                pl.BlockSpec((peers, tile, 3 * local), lambda i, m: (0, i, 0)),
                pl.BlockSpec((peers, tile, 2 * local), lambda i, m: (0, i, 0)),
            ],
        ),
        out_shape=[
            pltpu.HBM((peers, rows, 3 * local), lead.dtype),
            pltpu.HBM((peers, rows, 2 * local), lead.dtype),
        ],
        compiler_params=PARAMS,
        name="assemble",
    )(me, lead, *parts)


def unpack_kernel(part_ref, out_ref):
    peers, _, local = part_ref.shape
    for j in range(peers):
        out_ref[:, j * local : (j + 1) * local] = part_ref[j]


def unpack(parts):
    peers, rows, local = parts.shape
    tile = rows // PACK_STEPS
    return pl.pallas_call(
        unpack_kernel,
        grid=(PACK_STEPS,),
        in_specs=[pl.BlockSpec((peers, tile, local), lambda i: (0, i, 0))],
        out_specs=pl.BlockSpec((tile, peers * local), lambda i: (i, 0)),
        out_shape=jax.ShapeDtypeStruct((rows, peers * local), parts.dtype),
        compiler_params=PARAMS,
        name="unpack",
    )(parts)


def select_kernel(pick_ref, *refs):
    out_ref = refs[-1]
    base = pl.program_id(0) * out_ref.shape[0]
    for i in range(out_ref.shape[0]):
        for g, kv_ref in enumerate(refs[:-1]):
            out_ref[i, :, 2 * g * HDIM : 2 * (g + 1) * HDIM] = kv_ref[pick_ref[base + i]]


def select_blocks(picks, blocks, heads):
    frames = picks.shape[0]
    step = frames // SELECT_STEPS
    count, rows, _ = blocks.shape
    width = 2 * HDIM * len(heads)
    return pl.pallas_call(
        select_kernel,
        grid_spec=pltpu.PrefetchScalarGridSpec(
            num_scalar_prefetch=1,
            grid=(SELECT_STEPS,),
            in_specs=[
                pl.BlockSpec((count, rows, 2 * HDIM), lambda i, p, h=h: (0, 0, h)) for h in heads
            ],
            out_specs=pl.BlockSpec((step, rows, width), lambda i, p: (i, 0, 0)),
        ),
        out_shape=pltpu.HBM((frames, rows, width), blocks.dtype),
        compiler_params=PARAMS,
        name="select",
    )(picks, *([blocks] * len(heads)))


def near_kernel(on_ref, q_ref, own_ref, before_ref, after_ref, o_ref, m_ref, l_ref):
    tile = q_ref.shape[0]
    sub = tile // BLOCK
    first = pl.program_id(1) * sub
    query = q_ref[...]
    parts = [dot(query, own_ref[:, :HDIM], NT)]
    for side, ref in enumerate((before_ref, after_ref)):
        scores = dot(query, ref[:, :HDIM], NT)
        rows = []
        for s in range(sub):
            cols = []
            for b in range(BF):
                bias = jnp.where(on_ref[first + s, side * BF + b] > 0, 0.0, NEG)
                cols.append(
                    scores[s * BLOCK : (s + 1) * BLOCK, b * BLOCK : (b + 1) * BLOCK] + bias
                )
            rows.append(jnp.concatenate(cols, axis=1))
        parts.append(jnp.concatenate(rows, axis=0))
    top = functools.reduce(jnp.maximum, [jnp.max(p, axis=1, keepdims=True) for p in parts])
    mass = jnp.zeros((tile, HDIM), jnp.float32)
    summed = jnp.zeros((tile, HDIM), jnp.float32)
    for part, ref in zip(parts, (own_ref, before_ref, after_ref)):
        weights = jnp.exp2((part - top) * SCALE2)
        for b in range(BF):
            mass = mass + weights[:, b * BLOCK : (b + 1) * BLOCK]
        summed = summed + dot(weights.astype(jnp.bfloat16), ref[:, HDIM:], NN)
    o_ref[...] = summed
    m_ref[...] = jnp.broadcast_to(top, (tile, HDIM))
    l_ref[...] = mass


def near_attention(near_on, mixed, before, after):
    tile = 256
    rows, width = mixed.shape
    heads = HEADS_LOCAL
    first = width // HDIM - heads
    whole = pl.BlockSpec((rows, 2 * HDIM), lambda h, i, on: (0, h))
    return pl.pallas_call(
        near_kernel,
        grid_spec=pltpu.PrefetchScalarGridSpec(
            num_scalar_prefetch=1,
            grid=(heads, rows // tile),
            in_specs=[
                pl.BlockSpec((tile, HDIM), lambda h, i, on: (i, first + h)),
                whole,
                whole,
                whole,
            ],
            out_specs=[pl.BlockSpec((tile, HDIM), lambda h, i, on: (i, h))] * 3,
        ),
        out_shape=[pltpu.HBM((rows, heads * HDIM), jnp.float32)] * 3,
        cost_estimate=pl.CostEstimate(
            flops=12 * heads * rows * rows * HDIM,
            bytes_accessed=8 * heads * rows * 2 * HDIM,
            transcendentals=3 * heads * rows * rows,
        ),
        compiler_params=PARAMS,
        name="near",
    )(near_on, mixed, mixed, before, after)


def far_kernel(list_ref, count_ref, q_ref, kv_ref, o_ref, m_ref, l_ref, *refs):
    out_ref, m_s, l_s, acc_s = refs[-4:]
    m_s[...] = m_ref[...]
    l_s[...] = l_ref[...]
    acc_s[...] = o_ref[...]
    blocks = q_ref.shape[0] // BLOCK
    most = count_ref[0]
    for qb in range(1, blocks):
        most = jnp.maximum(most, count_ref[qb])

    def step(t, carry):
        for qb in range(blocks):
            rows = slice(qb * BLOCK, (qb + 1) * BLOCK)
            query = q_ref[rows, :]
            frames = [list_ref[qb, t * GROUP + i] for i in range(GROUP)]
            keys = jnp.concatenate([kv_ref[f, :, :HDIM] for f in frames], axis=0)
            values = jnp.concatenate([kv_ref[f, :, HDIM:] for f in frames], axis=0)
            raw = dot(query, keys, NT)
            scores = []
            for i in range(GROUP):
                bias = jnp.where(t * GROUP + i < count_ref[qb], 0.0, NEG)
                scores.append(raw[:, i * BLOCK : (i + 1) * BLOCK] + bias)
            old = m_s[rows, :]
            peak = functools.reduce(jnp.maximum, scores)
            top = jnp.maximum(old, jnp.max(peak, axis=1, keepdims=True))
            fade = jnp.exp2((old - top) * SCALE2)
            weights = [jnp.exp2((s - top) * SCALE2) for s in scores]
            rounded = jnp.concatenate([w.astype(jnp.bfloat16) for w in weights], axis=1)
            m_s[rows, :] = top
            l_s[rows, :] = l_s[rows, :] * fade + functools.reduce(jnp.add, weights)
            acc_s[rows, :] = acc_s[rows, :] * fade + dot(rounded, values, NN)
        return carry

    lax.fori_loop(0, (most + GROUP - 1) // GROUP, step, 0)
    total = jnp.sum(l_s[...], axis=1, keepdims=True)
    out_ref[...] = (acc_s[...] / total).astype(out_ref.dtype)


def far_attention(order, counts, mixed, heads, far, near, result):
    rows, width = mixed.shape
    column = width // HDIM - HEADS_LOCAL + heads[0]
    first = heads[0]
    frames = far.shape[0]
    full = pl.BlockSpec((rows, HDIM), lambda g, a, b: (0, first + g))
    operands = [order, counts, mixed, far, *in_hbm(*near)] + ([] if result is None else [result])
    return pl.pallas_call(
        far_kernel,
        grid_spec=pltpu.PrefetchScalarGridSpec(
            num_scalar_prefetch=2,
            grid=(len(heads),),
            in_specs=[
                pl.BlockSpec((rows, HDIM), lambda g, a, b: (0, column + g)),
                pl.BlockSpec((frames, BLOCK, 2 * HDIM), lambda g, a, b: (0, 0, g)),
                full,
                full,
                full,
            ]
            + ([] if result is None else [pl.BlockSpec(memory_space=pl.ANY)]),
            out_specs=full,
            scratch_shapes=[
                pltpu.VMEM((rows, HDIM), jnp.float32),
                pltpu.VMEM((rows, HDIM), jnp.float32),
                pltpu.VMEM((rows, HDIM), jnp.float32),
            ],
        ),
        out_shape=pltpu.HBM((rows, HEADS_LOCAL * HDIM), mixed.dtype),
        input_output_aliases={} if result is None else {7: 0},
        cost_estimate=pl.CostEstimate(
            flops=len(heads) * rows * frames * BLOCK * HDIM,
            bytes_accessed=len(heads) * frames * BLOCK * 2 * HDIM * 2,
            transcendentals=len(heads) * rows * frames * BLOCK // 4,
        ),
        compiler_params=PARAMS,
        name="far",
    )(*operands)


def mask_tables(block_mask, frame_id, frame_count):
    block_ids = jnp.arange(BF, dtype=jnp.int32)
    frame_ids = jnp.arange(frame_count, dtype=jnp.int32)
    towards = lax.dynamic_slice_in_dim(block_mask, frame_id * BF, BF, 1)
    towards = jnp.max(towards.reshape(frame_count, BF, BF), axis=1)
    outgoing = jnp.minimum(jnp.sum(towards * block_ids[None, :], axis=1), BF - 1)
    own = lax.dynamic_slice_in_dim(block_mask, frame_id * BF, BF, 0)
    padded = jnp.pad(own, ((0, 0), (BF, BF)))
    beside = lax.dynamic_slice_in_dim(padded, frame_id * BF, 3 * BF, 1)
    near_on = jnp.concatenate([beside[:, :BF], beside[:, 2 * BF :]], axis=1)
    distant = (jnp.abs(frame_ids - frame_id) >= 2).astype(jnp.int32)
    active = jnp.max(own.reshape(BF, frame_count, BF), axis=2) * distant[None, :]
    upto = (frame_ids[:, None] <= frame_ids[None, :]).astype(jnp.int32)
    place = jnp.sum(active[:, :, None] * upto[None, :, :], axis=1)
    counts = jnp.sum(active, axis=1)
    slots = jnp.where(active > 0, place - 1, -1)
    hit = (slots[:, :, None] == frame_ids[None, None, :]).astype(jnp.int32)
    order = jnp.sum(hit * frame_ids[None, :, None], axis=1)
    return outgoing, near_on, order, counts


def body(queries, key_rows, value_rows, block_mask):
    frame_count = lax.axis_size("frame")
    peers = lax.axis_size("head")
    frame_id = lax.axis_index("frame")
    me = lax.axis_index("head").astype(jnp.int32).reshape(1)
    exchange = functools.partial(lax.all_to_all, split_axis=0, concat_axis=0, tiled=True)
    up = [(i, i + 1) for i in range(frame_count - 1)]
    down = [(j, i) for i, j in up]
    early, late = [0], list(range(1, HEADS_LOCAL))
    outgoing, near_on, order, counts = mask_tables(block_mask, frame_id, frame_count)
    lead = exchange(pack_lead(key_rows, value_rows, peers), "head")
    parts = pack_rest(me, queries, key_rows, value_rows, peers)
    parcel = select_blocks(outgoing, lead, early)
    far_early = exchange(parcel, "frame")
    moved = [parts[0]]
    for d in range(1, peers):
        turn = [(i, (i + d) % peers) for i in range(peers)]
        moved.append(lax.ppermute(parts[d], "head", turn))
    blocks, pairs = assemble(me, lead, moved)
    mixed = blocks.reshape(FT, blocks.shape[2])
    pairs = pairs.reshape(FT, pairs.shape[2])
    parcel = select_blocks(outgoing, blocks, late)
    far_late = exchange(parcel, "frame")
    before = lax.ppermute(pairs, "frame", up)
    after = lax.ppermute(pairs, "frame", down)
    near = near_attention(near_on, mixed, before, after)
    result = far_attention(order, counts, mixed, early, far_early, near, None)
    result = far_attention(order, counts, mixed, late, far_late, near, result)
    result = result.reshape(peers, BLOCK, HEADS_LOCAL * HDIM)
    return unpack(exchange(result, "head"))


def solution(mesh):
    placed = (
        P(("frame", "head"), None),
        P(("frame", "head"), None),
        P(("frame", "head"), None),
        P(),
    )
    return jax.shard_map(
        body, mesh=mesh, in_specs=placed, out_specs=P(("frame", "head"), None), check_vma=False
    )
```

```python
import functools
import math

import jax
import jax.numpy as jnp
from jax import lax
from jax.experimental import pallas as pl
from jax.experimental.pallas import tpu as pltpu
from jax.sharding import PartitionSpec as P

HDIM = 128
BLOCK = 128
BF = 8
FT = BF * BLOCK
HEADS_LOCAL = 3
GROUP = 4
TEAM = 4
PACK_STEPS = 4
SELECT_STEPS = 2
PARAMS = pltpu.CompilerParams(vmem_limit_bytes=24 << 20)
NEG = -1e30
SCALE2 = math.log2(math.e) / math.sqrt(HDIM)
NT = (((1,), (1,)), ((), ()))
NN = (((1,), (0,)), ((), ()))


def in_hbm(*arrays):
    return [pltpu.with_memory_space_constraint(a, pltpu.HBM) for a in arrays]


def dot(a, b, dims):
    return lax.dot_general(a, b, dims, preferred_element_type=jnp.float32)


def lead_kernel(k_ref, v_ref, out_ref):
    peers = out_ref.shape[0]
    local = k_ref.shape[1] // peers
    for j in range(peers):
        out_ref[j, :, :HDIM] = k_ref[:, j * local : j * local + HDIM]
        out_ref[j, :, HDIM:] = v_ref[:, j * local : j * local + HDIM]


def pack_lead(keys, values, peers):
    rows, width = keys.shape
    tile = rows // PACK_STEPS
    spec = pl.BlockSpec((tile, width), lambda i: (i, 0))
    return pl.pallas_call(
        lead_kernel,
        grid=(PACK_STEPS,),
        in_specs=[spec] * 2,
        out_specs=pl.BlockSpec((peers, tile, 2 * HDIM), lambda i: (0, i, 0)),
        out_shape=pltpu.HBM((peers, rows, 2 * HDIM), keys.dtype),
        compiler_params=PARAMS,
        name="lead",
    )(*in_hbm(keys, values))


def rest_kernel(me_ref, q_ref, k_ref, v_ref, *out_refs):
    peers = len(out_refs)
    local = q_ref.shape[1] // peers
    heads = local // HDIM
    for d, out_ref in enumerate(out_refs):
        base = lax.rem(me_ref[0] + d, peers) * local
        for h in range(1, heads):
            cols = pl.ds(pl.multiple_of(base + h * HDIM, HDIM), HDIM)
            left = 2 * (h - 1) * HDIM
            out_ref[:, left : left + HDIM] = k_ref[:, cols]
            out_ref[:, left + HDIM : left + 2 * HDIM] = v_ref[:, cols]
        left = 2 * (heads - 1) * HDIM
        for h in range(heads):
            cols = pl.ds(pl.multiple_of(base + h * HDIM, HDIM), HDIM)
            out_ref[:, left + h * HDIM : left + (h + 1) * HDIM] = q_ref[:, cols]


def pack_rest(me, queries, keys, values, peers):
    rows, width = queries.shape
    local = width // peers
    size = 3 * local - 2 * HDIM
    tile = rows // PACK_STEPS
    spec = pl.BlockSpec((tile, width), lambda i, m: (i, 0))
    return pl.pallas_call(
        rest_kernel,
        grid_spec=pltpu.PrefetchScalarGridSpec(
            num_scalar_prefetch=1,
            grid=(PACK_STEPS,),
            in_specs=[spec] * 3,
            out_specs=[pl.BlockSpec((tile, size), lambda i, m: (i, 0))] * peers,
        ),
        out_shape=[pltpu.HBM((rows, size), queries.dtype)] * peers,
        compiler_params=PARAMS,
        name="rest",
    )(me, *in_hbm(queries, keys, values))


def gather_kernel(me_ref, lead_ref, *refs):
    parts, (mixed_ref, pairs_ref) = refs[:-2], refs[-2:]
    peers = len(parts)
    split = pairs_ref.shape[2]
    mixed_ref[:, :, : 2 * HDIM] = lead_ref[...]
    for d, ref in enumerate(parts):
        block = lax.rem(me_ref[0] - d + peers, peers)
        part = ref[...]
        mixed_ref[block, :, 2 * HDIM :] = part
        pairs_ref[block] = part[:, :split]


def assemble(me, lead, parts):
    peers, rows, _ = lead.shape
    size = parts[0].shape[1]
    local = (size + 2 * HDIM) // 3
    tile = rows // PACK_STEPS
    return pl.pallas_call(
        gather_kernel,
        grid_spec=pltpu.PrefetchScalarGridSpec(
            num_scalar_prefetch=1,
            grid=(PACK_STEPS,),
            in_specs=[pl.BlockSpec((peers, tile, 2 * HDIM), lambda i, m: (0, i, 0))]
            + [pl.BlockSpec((tile, size), lambda i, m: (i, 0))] * peers,
            out_specs=[
                pl.BlockSpec((peers, tile, 3 * local), lambda i, m: (0, i, 0)),
                pl.BlockSpec((peers, tile, 2 * local - 2 * HDIM), lambda i, m: (0, i, 0)),
            ],
        ),
        out_shape=[
            pltpu.HBM((peers, rows, 3 * local), lead.dtype),
            pltpu.HBM((peers, rows, 2 * local - 2 * HDIM), lead.dtype),
        ],
        compiler_params=PARAMS,
        name="assemble",
    )(me, lead, *parts)


def unpack_kernel(part_ref, out_ref):
    peers, _, local = part_ref.shape
    for j in range(peers):
        out_ref[:, j * local : (j + 1) * local] = part_ref[j]


def unpack(parts):
    peers, rows, local = parts.shape
    tile = rows // PACK_STEPS
    return pl.pallas_call(
        unpack_kernel,
        grid=(PACK_STEPS,),
        in_specs=[pl.BlockSpec((peers, tile, local), lambda i: (0, i, 0))],
        out_specs=pl.BlockSpec((tile, peers * local), lambda i: (i, 0)),
        out_shape=jax.ShapeDtypeStruct((rows, peers * local), parts.dtype),
        compiler_params=PARAMS,
        name="unpack",
    )(parts)


def select_kernel(pick_ref, *refs):
    out_ref = refs[-1]
    base = pl.program_id(0) * out_ref.shape[0]
    for i in range(out_ref.shape[0]):
        for g, kv_ref in enumerate(refs[:-1]):
            out_ref[i, :, 2 * g * HDIM : 2 * (g + 1) * HDIM] = kv_ref[pick_ref[base + i]]


def select_blocks(picks, blocks, heads):
    frames = picks.shape[0]
    step = frames // SELECT_STEPS
    count, rows, _ = blocks.shape
    width = 2 * HDIM * len(heads)
    return pl.pallas_call(
        select_kernel,
        grid_spec=pltpu.PrefetchScalarGridSpec(
            num_scalar_prefetch=1,
            grid=(SELECT_STEPS,),
            in_specs=[
                pl.BlockSpec((count, rows, 2 * HDIM), lambda i, p, h=h: (0, 0, h)) for h in heads
            ],
            out_specs=pl.BlockSpec((step, rows, width), lambda i, p: (i, 0, 0)),
        ),
        out_shape=pltpu.HBM((frames, rows, width), blocks.dtype),
        compiler_params=PARAMS,
        name="select",
    )(picks, *([blocks] * len(heads)))


def near_kernel(on_ref, q_ref, own_ref, before_ref, after_ref, o_ref, m_ref, l_ref):
    tile = q_ref.shape[0]
    sub = tile // BLOCK
    first = pl.program_id(1) * sub
    query = q_ref[...]
    parts = [dot(query, own_ref[:, :HDIM], NT)]
    for side, ref in enumerate((before_ref, after_ref)):
        scores = dot(query, ref[:, :HDIM], NT)
        rows = []
        for s in range(sub):
            cols = []
            for b in range(BF):
                bias = jnp.where(on_ref[first + s, side * BF + b] > 0, 0.0, NEG)
                cols.append(
                    scores[s * BLOCK : (s + 1) * BLOCK, b * BLOCK : (b + 1) * BLOCK] + bias
                )
            rows.append(jnp.concatenate(cols, axis=1))
        parts.append(jnp.concatenate(rows, axis=0))
    top = functools.reduce(jnp.maximum, [jnp.max(p, axis=1, keepdims=True) for p in parts])
    mass = jnp.zeros((tile, HDIM), jnp.float32)
    summed = jnp.zeros((tile, HDIM), jnp.float32)
    for part, ref in zip(parts, (own_ref, before_ref, after_ref)):
        weights = jnp.exp2((part - top) * SCALE2)
        for b in range(BF):
            mass = mass + weights[:, b * BLOCK : (b + 1) * BLOCK]
        summed = summed + dot(weights.astype(jnp.bfloat16), ref[:, HDIM:], NN)
    o_ref[...] = summed
    m_ref[...] = jnp.broadcast_to(top, (tile, HDIM))
    l_ref[...] = mass


def near_attention(near_on, mixed, group, before, after):
    tile = 256
    rows, width = mixed.shape
    heads = len(group)
    start = group[0]
    first = width // HDIM - HEADS_LOCAL + start
    whole = pl.BlockSpec((rows, 2 * HDIM), lambda h, i, on: (0, h))
    return pl.pallas_call(
        near_kernel,
        grid_spec=pltpu.PrefetchScalarGridSpec(
            num_scalar_prefetch=1,
            grid=(heads, rows // tile),
            in_specs=[
                pl.BlockSpec((tile, HDIM), lambda h, i, on: (i, first + h)),
                pl.BlockSpec((rows, 2 * HDIM), lambda h, i, on: (0, start + h)),
                whole,
                whole,
            ],
            out_specs=[pl.BlockSpec((tile, HDIM), lambda h, i, on: (i, h))] * 3,
        ),
        out_shape=[pltpu.HBM((rows, heads * HDIM), jnp.float32)] * 3,
        cost_estimate=pl.CostEstimate(
            flops=12 * heads * rows * rows * HDIM,
            bytes_accessed=8 * heads * rows * 2 * HDIM,
            transcendentals=3 * heads * rows * rows,
        ),
        compiler_params=PARAMS,
        name="near",
    )(near_on, mixed, mixed, before, after)


def far_kernel(list_ref, rank_ref, count_ref, q_ref, kv_ref, o_ref, m_ref, l_ref, *refs):
    out_ref, m_s, l_s, acc_s = refs[-4:]
    m_s[...] = m_ref[...]
    l_s[...] = l_ref[...]
    acc_s[...] = o_ref[...]
    blocks = q_ref.shape[0] // BLOCK

    def step(lead, t, carry):
        units = []
        for s in range(lead, lead + TEAM):
            qb = rank_ref[s]
            rows = pl.ds(pl.multiple_of(qb * BLOCK, BLOCK), BLOCK)
            frames = [list_ref[qb, t * GROUP + i] for i in range(GROUP)]
            keys = jnp.concatenate([kv_ref[f, :, :HDIM] for f in frames], axis=0)
            raw = dot(q_ref[rows, :], keys, NT)
            units.append((qb, rows, frames, raw, m_s[rows, :], l_s[rows, :], acc_s[rows, :]))
        soft = []
        for qb, rows, frames, raw, old, mass, acc in units:
            scores = []
            for i in range(GROUP):
                bias = jnp.where(t * GROUP + i < count_ref[qb], 0.0, NEG)
                scores.append(raw[:, i * BLOCK : (i + 1) * BLOCK] + bias)
            peak = functools.reduce(jnp.maximum, scores)
            top = jnp.maximum(old, jnp.max(peak, axis=1, keepdims=True))
            fade = jnp.exp2((old - top) * SCALE2)
            weights = [jnp.exp2((s - top) * SCALE2) for s in scores]
            rounded = jnp.concatenate([w.astype(jnp.bfloat16) for w in weights], axis=1)
            mass = mass * fade + functools.reduce(jnp.add, weights)
            soft.append((rows, frames, top, mass, acc * fade, rounded))
        done = []
        for rows, frames, top, mass, acc, rounded in soft:
            values = jnp.concatenate([kv_ref[f, :, HDIM:] for f in frames], axis=0)
            done.append((rows, top, mass, acc + dot(rounded, values, NN)))
        for rows, top, mass, acc in done:
            m_s[rows, :] = top
            l_s[rows, :] = mass
            acc_s[rows, :] = acc
        return carry

    for lead in range(0, blocks, TEAM):
        trips = (count_ref[rank_ref[lead]] + GROUP - 1) // GROUP
        lax.fori_loop(0, trips, functools.partial(step, lead), 0)
    total = jnp.sum(l_s[...], axis=1, keepdims=True)
    out_ref[...] = (acc_s[...] / total).astype(out_ref.dtype)


def far_attention(tables, mixed, heads, far, near, result):
    rows, width = mixed.shape
    column = width // HDIM - HEADS_LOCAL + heads[0]
    first = heads[0]
    frames = far.shape[0]
    full = pl.BlockSpec((rows, HDIM), lambda g, a, b, c: (0, g))
    operands = [*tables, mixed, far, *in_hbm(*near)] + ([] if result is None else [result])
    return pl.pallas_call(
        far_kernel,
        grid_spec=pltpu.PrefetchScalarGridSpec(
            num_scalar_prefetch=3,
            grid=(len(heads),),
            in_specs=[
                pl.BlockSpec((rows, HDIM), lambda g, a, b, c: (0, column + g)),
                pl.BlockSpec((frames, BLOCK, 2 * HDIM), lambda g, a, b, c: (0, 0, g)),
                full,
                full,
                full,
            ]
            + ([] if result is None else [pl.BlockSpec(memory_space=pl.ANY)]),
            out_specs=pl.BlockSpec((rows, HDIM), lambda g, a, b, c: (0, first + g)),
            scratch_shapes=[
                pltpu.VMEM((rows, HDIM), jnp.float32),
                pltpu.VMEM((rows, HDIM), jnp.float32),
                pltpu.VMEM((rows, HDIM), jnp.float32),
            ],
        ),
        out_shape=pltpu.HBM((rows, HEADS_LOCAL * HDIM), mixed.dtype),
        input_output_aliases={} if result is None else {8: 0},
        cost_estimate=pl.CostEstimate(
            flops=len(heads) * rows * frames * BLOCK * HDIM,
            bytes_accessed=len(heads) * frames * BLOCK * 2 * HDIM * 2,
            transcendentals=len(heads) * rows * frames * BLOCK // 4,
        ),
        compiler_params=PARAMS,
        name="far",
    )(*operands)


def mask_tables(block_mask, frame_id, frame_count):
    block_ids = jnp.arange(BF, dtype=jnp.int32)
    frame_ids = jnp.arange(frame_count, dtype=jnp.int32)
    towards = lax.dynamic_slice_in_dim(block_mask, frame_id * BF, BF, 1)
    towards = jnp.max(towards.reshape(frame_count, BF, BF), axis=1)
    outgoing = jnp.minimum(jnp.sum(towards * block_ids[None, :], axis=1), BF - 1)
    own = lax.dynamic_slice_in_dim(block_mask, frame_id * BF, BF, 0)
    padded = jnp.pad(own, ((0, 0), (BF, BF)))
    beside = lax.dynamic_slice_in_dim(padded, frame_id * BF, 3 * BF, 1)
    near_on = jnp.concatenate([beside[:, :BF], beside[:, 2 * BF :]], axis=1)
    distant = (jnp.abs(frame_ids - frame_id) >= 2).astype(jnp.int32)
    active = jnp.max(own.reshape(BF, frame_count, BF), axis=2) * distant[None, :]
    upto = (frame_ids[:, None] <= frame_ids[None, :]).astype(jnp.int32)
    place = jnp.sum(active[:, :, None] * upto[None, :, :], axis=1)
    counts = jnp.sum(active, axis=1)
    slots = jnp.where(active > 0, place - 1, -1)
    hit = (slots[:, :, None] == frame_ids[None, None, :]).astype(jnp.int32)
    order = jnp.sum(hit * frame_ids[None, :, None], axis=1)
    ids = block_ids
    ahead = (counts[None, :] > counts[:, None]) | (
        (counts[None, :] == counts[:, None]) & (ids[None, :] < ids[:, None])
    )
    seat = jnp.sum(ahead.astype(jnp.int32), axis=1)
    rank = jnp.sum((seat[:, None] == ids[None, :]).astype(jnp.int32) * ids[:, None], axis=0)
    return outgoing, near_on, (order, rank, counts)


def body(queries, key_rows, value_rows, block_mask):
    frame_count = lax.axis_size("frame")
    peers = lax.axis_size("head")
    frame_id = lax.axis_index("frame")
    me = lax.axis_index("head").astype(jnp.int32).reshape(1)
    exchange = functools.partial(lax.all_to_all, split_axis=0, concat_axis=0, tiled=True)
    up = [(i, i + 1) for i in range(frame_count - 1)]
    down = [(j, i) for i, j in up]
    early, late = [0], list(range(1, HEADS_LOCAL))
    outgoing, near_on, tables = mask_tables(block_mask, frame_id, frame_count)
    lead = exchange(pack_lead(key_rows, value_rows, peers), "head")
    parts = pack_rest(me, queries, key_rows, value_rows, peers)
    flat = lead.reshape(FT, lead.shape[2])
    before_early = lax.ppermute(flat, "frame", up)
    after_early = lax.ppermute(flat, "frame", down)
    parcel = select_blocks(outgoing, lead, early)
    far_early = exchange(parcel, "frame")
    moved = [parts[0]]
    for d in range(1, peers):
        turn = [(i, (i + d) % peers) for i in range(peers)]
        moved.append(lax.ppermute(parts[d], "head", turn))
    blocks, pairs = assemble(me, lead, moved)
    mixed = blocks.reshape(FT, blocks.shape[2])
    pairs = pairs.reshape(FT, pairs.shape[2])
    parcel = select_blocks(outgoing, blocks, late)
    far_late = exchange(parcel, "frame")
    before_late = lax.ppermute(pairs, "frame", up)
    after_late = lax.ppermute(pairs, "frame", down)
    near_early = near_attention(near_on, mixed, early, before_early, after_early)
    near_late = near_attention(near_on, mixed, late, before_late, after_late)
    result = far_attention(tables, mixed, early, far_early, near_early, None)
    result = far_attention(tables, mixed, late, far_late, near_late, result)
    result = result.reshape(peers, BLOCK, HEADS_LOCAL * HDIM)
    return unpack(exchange(result, "head"))


def solution(mesh):
    placed = (
        P(("frame", "head"), None),
        P(("frame", "head"), None),
        P(("frame", "head"), None),
        P(),
    )
    return jax.shard_map(
        body, mesh=mesh, in_specs=placed, out_specs=P(("frame", "head"), None), check_vma=False
    )
```

```python
import functools
import math

import jax
import jax.numpy as jnp
from jax import lax
from jax.experimental import pallas as pl
from jax.experimental.pallas import tpu as pltpu
from jax.sharding import PartitionSpec as P

HDIM = 128
BLOCK = 128
BF = 8
FT = BF * BLOCK
HEADS_LOCAL = 3
GROUP = 4
TEAM = 4
PACK_STEPS = 4
LEAD_STEPS = 2
JOIN_STEPS = 2
SELECT_STEPS = 2
PARAMS = pltpu.CompilerParams(vmem_limit_bytes=24 << 20)
NEG = -1e30
SCALE2 = math.log2(math.e) / math.sqrt(HDIM)
NT = (((1,), (1,)), ((), ()))
NN = (((1,), (0,)), ((), ()))


def in_hbm(*arrays):
    return [pltpu.with_memory_space_constraint(a, pltpu.HBM) for a in arrays]


def dot(a, b, dims):
    return lax.dot_general(a, b, dims, preferred_element_type=jnp.float32)


def lead_kernel(*refs):
    out_ref = refs[-1]
    group = out_ref.shape[0]
    for j in range(group):
        out_ref[j, :, :HDIM] = refs[j][...]
        out_ref[j, :, HDIM:] = refs[group + j][...]


def pack_lead(keys, values, peers):
    rows, width = keys.shape
    stride = width // peers // HDIM
    group = peers // LEAD_STEPS
    specs = [
        pl.BlockSpec((rows, HDIM), lambda i, j=j: (0, (i * group + j) * stride)) for j in range(group)
    ]
    keys, values = in_hbm(keys, values)
    return pl.pallas_call(
        lead_kernel,
        grid=(LEAD_STEPS,),
        in_specs=specs * 2,
        out_specs=pl.BlockSpec((group, rows, 2 * HDIM), lambda i: (i, 0, 0)),
        out_shape=pltpu.HBM((peers, rows, 2 * HDIM), keys.dtype),
        compiler_params=PARAMS,
        name="lead",
    )(*([keys] * group), *([values] * group))


def rest_kernel(me_ref, q_ref, k_ref, v_ref, *out_refs):
    peers = len(out_refs) // 2
    local = q_ref.shape[1] // peers
    heads = local // HDIM
    for d in range(peers):
        pair_ref, query_ref = out_refs[d], out_refs[peers + d]
        base = lax.rem(me_ref[0] + d, peers) * local
        for h in range(1, heads):
            cols = pl.ds(pl.multiple_of(base + h * HDIM, HDIM), HDIM)
            left = 2 * (h - 1) * HDIM
            pair_ref[:, left : left + HDIM] = k_ref[:, cols]
            pair_ref[:, left + HDIM : left + 2 * HDIM] = v_ref[:, cols]
        query_ref[...] = q_ref[:, pl.ds(pl.multiple_of(base, HDIM), local)]


def pack_rest(me, queries, keys, values, peers):
    rows, width = queries.shape
    local = width // peers
    tile = rows // PACK_STEPS
    spec = pl.BlockSpec((tile, width), lambda i, m: (i, 0))
    sizes = [2 * local - 2 * HDIM] * peers + [local] * peers
    outs = pl.pallas_call(
        rest_kernel,
        grid_spec=pltpu.PrefetchScalarGridSpec(
            num_scalar_prefetch=1,
            grid=(PACK_STEPS,),
            in_specs=[spec] * 3,
            out_specs=[pl.BlockSpec((tile, size), lambda i, m: (i, 0)) for size in sizes],
        ),
        out_shape=[pltpu.HBM((rows, size), queries.dtype) for size in sizes],
        compiler_params=PARAMS,
        name="rest",
    )(me, *in_hbm(queries, keys, values))
    return outs[:peers], outs[peers:]


def gather_kernel(me_ref, *refs):
    out_ref = refs[-1]
    peers = len(refs) - 1
    for d, ref in enumerate(refs[:-1]):
        out_ref[lax.rem(me_ref[0] - d + peers, peers)] = ref[...]


def assemble(me, parts):
    peers = len(parts)
    rows, size = parts[0].shape
    tile = rows // JOIN_STEPS
    return pl.pallas_call(
        gather_kernel,
        grid_spec=pltpu.PrefetchScalarGridSpec(
            num_scalar_prefetch=1,
            grid=(JOIN_STEPS,),
            in_specs=[pl.BlockSpec((tile, size), lambda i, m: (i, 0))] * peers,
            out_specs=pl.BlockSpec((peers, tile, size), lambda i, m: (0, i, 0)),
        ),
        out_shape=pltpu.HBM((peers, rows, size), parts[0].dtype),
        compiler_params=PARAMS,
        name="assemble",
    )(me, *parts)


def unpack_kernel(part_ref, out_ref):
    peers, _, local = part_ref.shape
    for j in range(peers):
        out_ref[:, j * local : (j + 1) * local] = part_ref[j]


def unpack(parts):
    peers, rows, local = parts.shape
    tile = rows // PACK_STEPS
    return pl.pallas_call(
        unpack_kernel,
        grid=(PACK_STEPS,),
        in_specs=[pl.BlockSpec((peers, tile, local), lambda i: (0, i, 0))],
        out_specs=pl.BlockSpec((tile, peers * local), lambda i: (i, 0)),
        out_shape=jax.ShapeDtypeStruct((rows, peers * local), parts.dtype),
        compiler_params=PARAMS,
        name="unpack",
    )(parts)


def select_kernel(pick_ref, *refs):
    out_ref = refs[-1]
    base = pl.program_id(0) * out_ref.shape[0]
    for i in range(out_ref.shape[0]):
        for g, kv_ref in enumerate(refs[:-1]):
            out_ref[i, :, 2 * g * HDIM : 2 * (g + 1) * HDIM] = kv_ref[pick_ref[base + i]]


def select_blocks(picks, blocks):
    frames = picks.shape[0]
    step = frames // SELECT_STEPS
    count, rows, width = blocks.shape
    heads = range(width // (2 * HDIM))
    return pl.pallas_call(
        select_kernel,
        grid_spec=pltpu.PrefetchScalarGridSpec(
            num_scalar_prefetch=1,
            grid=(SELECT_STEPS,),
            in_specs=[
                pl.BlockSpec((count, rows, 2 * HDIM), lambda i, p, h=h: (0, 0, h)) for h in heads
            ],
            out_specs=pl.BlockSpec((step, rows, width), lambda i, p: (i, 0, 0)),
        ),
        out_shape=pltpu.HBM((frames, rows, width), blocks.dtype),
        compiler_params=PARAMS,
        name="select",
    )(picks, *([blocks] * len(heads)))


def near_kernel(on_ref, q_ref, own_ref, before_ref, after_ref, o_ref, m_ref, l_ref):
    tile = q_ref.shape[0]
    sub = tile // BLOCK
    first = pl.program_id(1) * sub
    query = q_ref[...]
    parts = [dot(query, own_ref[:, :HDIM], NT)]
    for side, ref in enumerate((before_ref, after_ref)):
        scores = dot(query, ref[:, :HDIM], NT)
        rows = []
        for s in range(sub):
            cols = []
            for b in range(BF):
                bias = jnp.where(on_ref[first + s, side * BF + b] > 0, 0.0, NEG)
                cols.append(
                    scores[s * BLOCK : (s + 1) * BLOCK, b * BLOCK : (b + 1) * BLOCK] + bias
                )
            rows.append(jnp.concatenate(cols, axis=1))
        parts.append(jnp.concatenate(rows, axis=0))
    top = functools.reduce(jnp.maximum, [jnp.max(p, axis=1, keepdims=True) for p in parts])
    mass = jnp.zeros((tile, HDIM), jnp.float32)
    summed = jnp.zeros((tile, HDIM), jnp.float32)
    for part, ref in zip(parts, (own_ref, before_ref, after_ref)):
        weights = jnp.exp2((part - top) * SCALE2)
        for b in range(BF):
            mass = mass + weights[:, b * BLOCK : (b + 1) * BLOCK]
        summed = summed + dot(weights.astype(jnp.bfloat16), ref[:, HDIM:], NN)
    o_ref[...] = summed
    m_ref[...] = jnp.broadcast_to(top, (tile, HDIM))
    l_ref[...] = mass


def near_attention(near_on, query, group, own, before, after):
    tile = 256
    rows = query.shape[0]
    heads = len(group)
    first = group[0]
    whole = pl.BlockSpec((rows, 2 * HDIM), lambda h, i, on: (0, h))
    return pl.pallas_call(
        near_kernel,
        grid_spec=pltpu.PrefetchScalarGridSpec(
            num_scalar_prefetch=1,
            grid=(heads, rows // tile),
            in_specs=[
                pl.BlockSpec((tile, HDIM), lambda h, i, on: (i, first + h)),
                whole,
                whole,
                whole,
            ],
            out_specs=[pl.BlockSpec((tile, HDIM), lambda h, i, on: (i, h))] * 3,
        ),
        out_shape=[pltpu.HBM((rows, heads * HDIM), jnp.float32)] * 3,
        cost_estimate=pl.CostEstimate(
            flops=12 * heads * rows * rows * HDIM,
            bytes_accessed=8 * heads * rows * 2 * HDIM,
            transcendentals=3 * heads * rows * rows,
        ),
        compiler_params=PARAMS,
        name="near",
    )(near_on, query, own, before, after)


def far_kernel(list_ref, rank_ref, count_ref, q_ref, kv_ref, o_ref, m_ref, l_ref, *refs):
    out_ref, m_s, l_s, acc_s = refs[-4:]
    m_s[...] = m_ref[...]
    l_s[...] = l_ref[...]
    acc_s[...] = o_ref[...]
    blocks = q_ref.shape[0] // BLOCK

    def step(lead, t, carry):
        units = []
        for s in range(lead, lead + TEAM):
            qb = rank_ref[s]
            rows = pl.ds(pl.multiple_of(qb * BLOCK, BLOCK), BLOCK)
            frames = [list_ref[qb, t * GROUP + i] for i in range(GROUP)]
            keys = jnp.concatenate([kv_ref[f, :, :HDIM] for f in frames], axis=0)
            raw = dot(q_ref[rows, :], keys, NT)
            units.append((qb, rows, frames, raw, m_s[rows, :], l_s[rows, :], acc_s[rows, :]))
        soft = []
        for qb, rows, frames, raw, old, mass, acc in units:
            scores = []
            for i in range(GROUP):
                bias = jnp.where(t * GROUP + i < count_ref[qb], 0.0, NEG)
                scores.append(raw[:, i * BLOCK : (i + 1) * BLOCK] + bias)
            peak = functools.reduce(jnp.maximum, scores)
            top = jnp.maximum(old, jnp.max(peak, axis=1, keepdims=True))
            fade = jnp.exp2((old - top) * SCALE2)
            weights = [jnp.exp2((s - top) * SCALE2) for s in scores]
            rounded = jnp.concatenate([w.astype(jnp.bfloat16) for w in weights], axis=1)
            mass = mass * fade + functools.reduce(jnp.add, weights)
            soft.append((rows, frames, top, mass, acc * fade, rounded))
        done = []
        for rows, frames, top, mass, acc, rounded in soft:
            values = jnp.concatenate([kv_ref[f, :, HDIM:] for f in frames], axis=0)
            done.append((rows, top, mass, acc + dot(rounded, values, NN)))
        for rows, top, mass, acc in done:
            m_s[rows, :] = top
            l_s[rows, :] = mass
            acc_s[rows, :] = acc
        return carry

    for lead in range(0, blocks, TEAM):
        trips = (count_ref[rank_ref[lead]] + GROUP - 1) // GROUP
        lax.fori_loop(0, trips, functools.partial(step, lead), 0)
    total = jnp.sum(l_s[...], axis=1, keepdims=True)
    out_ref[...] = (acc_s[...] / total).astype(out_ref.dtype)


def far_attention(tables, query, heads, far, near, result):
    rows = query.shape[0]
    first = heads[0]
    frames = far.shape[0]
    full = pl.BlockSpec((rows, HDIM), lambda g, a, b, c: (0, g))
    operands = [*tables, query, far, *in_hbm(*near)] + ([] if result is None else [result])
    return pl.pallas_call(
        far_kernel,
        grid_spec=pltpu.PrefetchScalarGridSpec(
            num_scalar_prefetch=3,
            grid=(len(heads),),
            in_specs=[
                pl.BlockSpec((rows, HDIM), lambda g, a, b, c: (0, first + g)),
                pl.BlockSpec((frames, BLOCK, 2 * HDIM), lambda g, a, b, c: (0, 0, g)),
                full,
                full,
                full,
            ]
            + ([] if result is None else [pl.BlockSpec(memory_space=pl.ANY)]),
            out_specs=pl.BlockSpec((rows, HDIM), lambda g, a, b, c: (0, first + g)),
            scratch_shapes=[
                pltpu.VMEM((rows, HDIM), jnp.float32),
                pltpu.VMEM((rows, HDIM), jnp.float32),
                pltpu.VMEM((rows, HDIM), jnp.float32),
            ],
        ),
        out_shape=pltpu.HBM((rows, HEADS_LOCAL * HDIM), query.dtype),
        input_output_aliases={} if result is None else {8: 0},
        cost_estimate=pl.CostEstimate(
            flops=len(heads) * rows * frames * BLOCK * HDIM,
            bytes_accessed=len(heads) * frames * BLOCK * 2 * HDIM * 2,
            transcendentals=len(heads) * rows * frames * BLOCK // 4,
        ),
        compiler_params=PARAMS,
        name="far",
    )(*operands)


def mask_tables(block_mask, frame_id, frame_count):
    block_ids = jnp.arange(BF, dtype=jnp.int32)
    frame_ids = jnp.arange(frame_count, dtype=jnp.int32)
    towards = lax.dynamic_slice_in_dim(block_mask, frame_id * BF, BF, 1)
    towards = jnp.max(towards.reshape(frame_count, BF, BF), axis=1)
    outgoing = jnp.minimum(jnp.sum(towards * block_ids[None, :], axis=1), BF - 1)
    own = lax.dynamic_slice_in_dim(block_mask, frame_id * BF, BF, 0)
    padded = jnp.pad(own, ((0, 0), (BF, BF)))
    beside = lax.dynamic_slice_in_dim(padded, frame_id * BF, 3 * BF, 1)
    near_on = jnp.concatenate([beside[:, :BF], beside[:, 2 * BF :]], axis=1)
    distant = (jnp.abs(frame_ids - frame_id) >= 2).astype(jnp.int32)
    active = jnp.max(own.reshape(BF, frame_count, BF), axis=2) * distant[None, :]
    upto = (frame_ids[:, None] <= frame_ids[None, :]).astype(jnp.int32)
    place = jnp.sum(active[:, :, None] * upto[None, :, :], axis=1)
    counts = jnp.sum(active, axis=1)
    slots = jnp.where(active > 0, place - 1, -1)
    hit = (slots[:, :, None] == frame_ids[None, None, :]).astype(jnp.int32)
    order = jnp.sum(hit * frame_ids[None, :, None], axis=1)
    ids = block_ids
    ahead = (counts[None, :] > counts[:, None]) | (
        (counts[None, :] == counts[:, None]) & (ids[None, :] < ids[:, None])
    )
    seat = jnp.sum(ahead.astype(jnp.int32), axis=1)
    rank = jnp.sum((seat[:, None] == ids[None, :]).astype(jnp.int32) * ids[:, None], axis=0)
    return outgoing, near_on, (order, rank, counts)


def body(queries, key_rows, value_rows, block_mask):
    frame_count = lax.axis_size("frame")
    peers = lax.axis_size("head")
    frame_id = lax.axis_index("frame")
    me = lax.axis_index("head").astype(jnp.int32).reshape(1)
    exchange = functools.partial(lax.all_to_all, split_axis=0, concat_axis=0, tiled=True)
    up = [(i, i + 1) for i in range(frame_count - 1)]
    down = [(j, i) for i, j in up]

    def turned(parts):
        moved = [parts[0]]
        for d in range(1, peers):
            turn = [(i, (i + d) % peers) for i in range(peers)]
            moved.append(lax.ppermute(parts[d], "head", turn))
        return moved

    early, late = [0], list(range(1, HEADS_LOCAL))
    outgoing, near_on, tables = mask_tables(block_mask, frame_id, frame_count)
    lead = exchange(pack_lead(key_rows, value_rows, peers), "head")
    pair_parts, query_parts = pack_rest(me, queries, key_rows, value_rows, peers)
    parcel = select_blocks(outgoing, lead)
    far_early = exchange(parcel, "frame")
    flat = lead.reshape(FT, lead.shape[2])
    pairs = assemble(me, turned(pair_parts))
    parcel = select_blocks(outgoing, pairs)
    far_late = exchange(parcel, "frame")
    pairs = pairs.reshape(FT, pairs.shape[2])
    before_early = lax.ppermute(flat, "frame", up)
    after_early = lax.ppermute(flat, "frame", down)
    before_late = lax.ppermute(pairs, "frame", up)
    after_late = lax.ppermute(pairs, "frame", down)
    query = assemble(me, turned(query_parts))
    query = query.reshape(FT, query.shape[2])
    near_early = near_attention(near_on, query, early, flat, before_early, after_early)
    near_late = near_attention(near_on, query, late, pairs, before_late, after_late)
    result = far_attention(tables, query, early, far_early, near_early, None)
    result = far_attention(tables, query, late, far_late, near_late, result)
    result = result.reshape(peers, BLOCK, HEADS_LOCAL * HDIM)
    return unpack(exchange(result, "head"))


def solution(mesh):
    placed = (
        P(("frame", "head"), None),
        P(("frame", "head"), None),
        P(("frame", "head"), None),
        P(),
    )
    return jax.shard_map(
        body, mesh=mesh, in_specs=placed, out_specs=P(("frame", "head"), None), check_vma=False
    )
```

```python
import functools
import math

import jax
import jax.numpy as jnp
from jax import lax
from jax.experimental import pallas as pl
from jax.experimental.pallas import tpu as pltpu
from jax.sharding import PartitionSpec as P

HDIM = 128
BLOCK = 128
BF = 8
FT = BF * BLOCK
HEADS_LOCAL = 3
GROUP = 4
TEAM = 4
PACK_STEPS = 4
LEAD_STEPS = 2
JOIN_STEPS = 2
PARAMS = pltpu.CompilerParams(vmem_limit_bytes=24 << 20)
NEG = -1e30
SCALE2 = math.log2(math.e) / math.sqrt(HDIM)
NT = (((1,), (1,)), ((), ()))
NN = (((1,), (0,)), ((), ()))


def in_hbm(*arrays):
    return [pltpu.with_memory_space_constraint(a, pltpu.HBM) for a in arrays]


def dot(a, b, dims):
    return lax.dot_general(a, b, dims, preferred_element_type=jnp.float32)


def lead_kernel(*refs):
    out_ref = refs[-1]
    group = out_ref.shape[0]
    for j in range(group):
        out_ref[j, :, :HDIM] = refs[j][...]
        out_ref[j, :, HDIM:] = refs[group + j][...]


def pack_lead(keys, values, peers):
    rows, width = keys.shape
    stride = width // peers // HDIM
    group = peers // LEAD_STEPS
    specs = [
        pl.BlockSpec((rows, HDIM), lambda i, j=j: (0, (i * group + j) * stride)) for j in range(group)
    ]
    keys, values = in_hbm(keys, values)
    return pl.pallas_call(
        lead_kernel,
        grid=(LEAD_STEPS,),
        in_specs=specs * 2,
        out_specs=pl.BlockSpec((group, rows, 2 * HDIM), lambda i: (i, 0, 0)),
        out_shape=pltpu.HBM((peers, rows, 2 * HDIM), keys.dtype),
        compiler_params=PARAMS,
        name="lead",
    )(*([keys] * group), *([values] * group))


def rest_kernel(me_ref, q_ref, k_ref, v_ref, *out_refs):
    peers = len(out_refs) // 2
    local = q_ref.shape[1] // peers
    heads = local // HDIM
    for d in range(peers):
        pair_ref, query_ref = out_refs[d], out_refs[peers + d]
        base = lax.rem(me_ref[0] + d, peers) * local
        for h in range(1, heads):
            cols = pl.ds(pl.multiple_of(base + h * HDIM, HDIM), HDIM)
            left = 2 * (h - 1) * HDIM
            pair_ref[:, left : left + HDIM] = k_ref[:, cols]
            pair_ref[:, left + HDIM : left + 2 * HDIM] = v_ref[:, cols]
        query_ref[...] = q_ref[:, pl.ds(pl.multiple_of(base, HDIM), local)]


def pack_rest(me, queries, keys, values, peers):
    rows, width = queries.shape
    local = width // peers
    tile = rows // PACK_STEPS
    spec = pl.BlockSpec((tile, width), lambda i, m: (i, 0))
    sizes = [2 * local - 2 * HDIM] * peers + [local] * peers
    outs = pl.pallas_call(
        rest_kernel,
        grid_spec=pltpu.PrefetchScalarGridSpec(
            num_scalar_prefetch=1,
            grid=(PACK_STEPS,),
            in_specs=[spec] * 3,
            out_specs=[pl.BlockSpec((tile, size), lambda i, m: (i, 0)) for size in sizes],
        ),
        out_shape=[pltpu.HBM((rows, size), queries.dtype) for size in sizes],
        compiler_params=PARAMS,
        name="rest",
    )(me, *in_hbm(queries, keys, values))
    return outs[:peers], outs[peers:]


def gather_kernel(me_ref, *refs):
    out_ref = refs[-1]
    peers = len(refs) - 1
    for d, ref in enumerate(refs[:-1]):
        out_ref[lax.rem(me_ref[0] - d + peers, peers)] = ref[...]


def assemble(me, parts):
    peers = len(parts)
    rows, size = parts[0].shape
    tile = rows // JOIN_STEPS
    return pl.pallas_call(
        gather_kernel,
        grid_spec=pltpu.PrefetchScalarGridSpec(
            num_scalar_prefetch=1,
            grid=(JOIN_STEPS,),
            in_specs=[pl.BlockSpec((tile, size), lambda i, m: (i, 0))] * peers,
            out_specs=pl.BlockSpec((peers, tile, size), lambda i, m: (0, i, 0)),
        ),
        out_shape=pltpu.HBM((peers, rows, size), parts[0].dtype),
        compiler_params=PARAMS,
        name="assemble",
    )(me, *parts)


def unpack_kernel(early_ref, late_ref, out_ref, sem):
    peers = late_ref.shape[0]
    copies, left = [], 0
    for j in range(peers):
        for part, ref in enumerate((early_ref, late_ref)):
            cols = slice(left, left + ref.shape[2])
            left += ref.shape[2]
            copies.append(
                pltpu.make_async_copy(ref.at[j], out_ref.at[:, cols], sem.at[2 * j + part])
            )
    for copy in copies:
        copy.start()
    for copy in copies:
        copy.wait()


def unpack(early, late):
    peers, rows, width = late.shape
    return pl.pallas_call(
        unpack_kernel,
        in_specs=[pl.BlockSpec(memory_space=pltpu.VMEM)] * 2,
        out_specs=pl.BlockSpec(memory_space=pl.ANY),
        out_shape=pltpu.HBM((rows, peers * (early.shape[2] + width)), late.dtype),
        scratch_shapes=[pltpu.SemaphoreType.DMA((2 * peers,))],
        compiler_params=PARAMS,
        name="unpack",
    )(early, late)


def select_kernel(pick_ref, kv_ref, out_ref, sem):
    copies = [
        pltpu.make_async_copy(kv_ref.at[pick_ref[i]], out_ref.at[i], sem.at[i])
        for i in range(out_ref.shape[0])
    ]
    for copy in copies:
        copy.start()
    for copy in copies:
        copy.wait()


def select_blocks(picks, blocks):
    frames = picks.shape[0]
    _, rows, width = blocks.shape
    return pl.pallas_call(
        select_kernel,
        in_specs=[
            pl.BlockSpec(memory_space=pltpu.SMEM),
            pl.BlockSpec(memory_space=pltpu.VMEM),
        ],
        out_specs=pl.BlockSpec(memory_space=pl.ANY),
        out_shape=pltpu.HBM((frames, rows, width), blocks.dtype),
        scratch_shapes=[pltpu.SemaphoreType.DMA((frames,))],
        compiler_params=PARAMS,
        name="select",
    )(picks, blocks)


def near_kernel(on_ref, q_ref, own_ref, before_ref, after_ref, o_ref, m_ref, l_ref):
    tile = q_ref.shape[0]
    sub = tile // BLOCK
    first = pl.program_id(1) * sub
    query = q_ref[...]
    parts = [dot(query, own_ref[:, :HDIM], NT)]
    for side, ref in enumerate((before_ref, after_ref)):
        scores = dot(query, ref[:, :HDIM], NT)
        rows = []
        for s in range(sub):
            cols = []
            for b in range(BF):
                bias = jnp.where(on_ref[first + s, side * BF + b] > 0, 0.0, NEG)
                cols.append(
                    scores[s * BLOCK : (s + 1) * BLOCK, b * BLOCK : (b + 1) * BLOCK] + bias
                )
            rows.append(jnp.concatenate(cols, axis=1))
        parts.append(jnp.concatenate(rows, axis=0))
    top = functools.reduce(jnp.maximum, [jnp.max(p, axis=1, keepdims=True) for p in parts])
    mass = jnp.zeros((tile, HDIM), jnp.float32)
    summed = jnp.zeros((tile, HDIM), jnp.float32)
    for part, ref in zip(parts, (own_ref, before_ref, after_ref)):
        weights = jnp.exp2((part - top) * SCALE2)
        for b in range(BF):
            mass = mass + weights[:, b * BLOCK : (b + 1) * BLOCK]
        summed = summed + dot(weights.astype(jnp.bfloat16), ref[:, HDIM:], NN)
    o_ref[...] = summed
    m_ref[...] = jnp.broadcast_to(top, (tile, HDIM))
    l_ref[...] = mass


def near_attention(near_on, query, group, own, before, after):
    tile = 256
    rows = query.shape[0]
    heads = len(group)
    first = group[0]
    whole = pl.BlockSpec((rows, 2 * HDIM), lambda h, i, on: (0, h))
    return pl.pallas_call(
        near_kernel,
        grid_spec=pltpu.PrefetchScalarGridSpec(
            num_scalar_prefetch=1,
            grid=(heads, rows // tile),
            in_specs=[
                pl.BlockSpec((tile, HDIM), lambda h, i, on: (i, first + h)),
                whole,
                whole,
                whole,
            ],
            out_specs=[pl.BlockSpec((tile, HDIM), lambda h, i, on: (i, h))] * 3,
        ),
        out_shape=[pltpu.HBM((rows, heads * HDIM), jnp.float32)] * 3,
        cost_estimate=pl.CostEstimate(
            flops=12 * heads * rows * rows * HDIM,
            bytes_accessed=8 * heads * rows * 2 * HDIM,
            transcendentals=3 * heads * rows * rows,
        ),
        compiler_params=PARAMS,
        name="near",
    )(near_on, query, own, before, after)


def far_kernel(list_ref, rank_ref, count_ref, me_ref, q_ref, kv_ref, o_ref, m_ref, l_ref, *refs):
    out_refs, (m_s, l_s, acc_s) = refs[:-3], refs[-3:]
    m_s[...] = m_ref[...]
    l_s[...] = l_ref[...]
    acc_s[...] = o_ref[...]
    blocks = q_ref.shape[0] // BLOCK

    def step(lead, t, carry):
        units = []
        for s in range(lead, lead + TEAM):
            qb = rank_ref[s]
            rows = pl.ds(pl.multiple_of(qb * BLOCK, BLOCK), BLOCK)
            frames = [list_ref[qb, t * GROUP + i] for i in range(GROUP)]
            keys = jnp.concatenate([kv_ref[f, :, :HDIM] for f in frames], axis=0)
            raw = dot(q_ref[rows, :], keys, NT)
            units.append((qb, rows, frames, raw, m_s[rows, :], l_s[rows, :], acc_s[rows, :]))
        soft = []
        for qb, rows, frames, raw, old, mass, acc in units:
            scores = []
            for i in range(GROUP):
                bias = jnp.where(t * GROUP + i < count_ref[qb], 0.0, NEG)
                scores.append(raw[:, i * BLOCK : (i + 1) * BLOCK] + bias)
            peak = functools.reduce(jnp.maximum, scores)
            top = jnp.maximum(old, jnp.max(peak, axis=1, keepdims=True))
            fade = jnp.exp2((old - top) * SCALE2)
            weights = [jnp.exp2((s - top) * SCALE2) for s in scores]
            rounded = jnp.concatenate([w.astype(jnp.bfloat16) for w in weights], axis=1)
            mass = mass * fade + functools.reduce(jnp.add, weights)
            soft.append((rows, frames, top, mass, acc * fade, rounded))
        done = []
        for rows, frames, top, mass, acc, rounded in soft:
            values = jnp.concatenate([kv_ref[f, :, HDIM:] for f in frames], axis=0)
            done.append((rows, top, mass, acc + dot(rounded, values, NN)))
        for rows, top, mass, acc in done:
            m_s[rows, :] = top
            l_s[rows, :] = mass
            acc_s[rows, :] = acc
        return carry

    for lead in range(0, blocks, TEAM):
        trips = (count_ref[rank_ref[lead]] + GROUP - 1) // GROUP
        lax.fori_loop(0, trips, functools.partial(step, lead), 0)
    peers = len(out_refs)
    for d, out_ref in enumerate(out_refs):
        rows = slice(None)
        if peers > 1:
            block = lax.rem(me_ref[0] + d, peers)
            rows = pl.ds(pl.multiple_of(block * BLOCK, BLOCK), BLOCK)
        total = jnp.sum(l_s[rows, :], axis=1, keepdims=True)
        out_ref[...] = (acc_s[rows, :] / total).astype(out_ref.dtype)


def far_attention(tables, me, query, heads, far, near, pieces):
    rows = query.shape[0]
    first = heads[0]
    frames = far.shape[0]
    full = pl.BlockSpec((rows, HDIM), lambda g, a, b, c, m: (0, g))
    out = pl.BlockSpec((rows // pieces, HDIM), lambda g, a, b, c, m: (0, g))
    return pl.pallas_call(
        far_kernel,
        grid_spec=pltpu.PrefetchScalarGridSpec(
            num_scalar_prefetch=4,
            grid=(len(heads),),
            in_specs=[
                pl.BlockSpec((rows, HDIM), lambda g, a, b, c, m: (0, first + g)),
                pl.BlockSpec((frames, BLOCK, 2 * HDIM), lambda g, a, b, c, m: (0, 0, g)),
                full,
                full,
                full,
            ],
            out_specs=[out] * pieces,
            scratch_shapes=[
                pltpu.VMEM((rows, HDIM), jnp.float32),
                pltpu.VMEM((rows, HDIM), jnp.float32),
                pltpu.VMEM((rows, HDIM), jnp.float32),
            ],
        ),
        out_shape=[pltpu.HBM((rows // pieces, len(heads) * HDIM), query.dtype)] * pieces,
        cost_estimate=pl.CostEstimate(
            flops=len(heads) * rows * frames * BLOCK * HDIM,
            bytes_accessed=len(heads) * frames * BLOCK * 2 * HDIM * 2,
            transcendentals=len(heads) * rows * frames * BLOCK // 4,
        ),
        compiler_params=PARAMS,
        name="far",
    )(*tables, me, query, far, *in_hbm(*near))


def mask_tables(block_mask, frame_id, frame_count):
    block_ids = jnp.arange(BF, dtype=jnp.int32)
    frame_ids = jnp.arange(frame_count, dtype=jnp.int32)
    towards = lax.dynamic_slice_in_dim(block_mask, frame_id * BF, BF, 1)
    towards = jnp.max(towards.reshape(frame_count, BF, BF), axis=1)
    outgoing = jnp.minimum(jnp.sum(towards * block_ids[None, :], axis=1), BF - 1)
    own = lax.dynamic_slice_in_dim(block_mask, frame_id * BF, BF, 0)
    padded = jnp.pad(own, ((0, 0), (BF, BF)))
    beside = lax.dynamic_slice_in_dim(padded, frame_id * BF, 3 * BF, 1)
    near_on = jnp.concatenate([beside[:, :BF], beside[:, 2 * BF :]], axis=1)
    distant = (jnp.abs(frame_ids - frame_id) >= 2).astype(jnp.int32)
    active = jnp.max(own.reshape(BF, frame_count, BF), axis=2) * distant[None, :]
    upto = (frame_ids[:, None] <= frame_ids[None, :]).astype(jnp.int32)
    place = jnp.sum(active[:, :, None] * upto[None, :, :], axis=1)
    counts = jnp.sum(active, axis=1)
    slots = jnp.where(active > 0, place - 1, -1)
    hit = (slots[:, :, None] == frame_ids[None, None, :]).astype(jnp.int32)
    order = jnp.sum(hit * frame_ids[None, :, None], axis=1)
    ids = block_ids
    ahead = (counts[None, :] > counts[:, None]) | (
        (counts[None, :] == counts[:, None]) & (ids[None, :] < ids[:, None])
    )
    seat = jnp.sum(ahead.astype(jnp.int32), axis=1)
    rank = jnp.sum((seat[:, None] == ids[None, :]).astype(jnp.int32) * ids[:, None], axis=0)
    return outgoing, near_on, (order, rank, counts)


def body(queries, key_rows, value_rows, block_mask):
    frame_count = lax.axis_size("frame")
    peers = lax.axis_size("head")
    frame_id = lax.axis_index("frame")
    me = lax.axis_index("head").astype(jnp.int32).reshape(1)
    exchange = functools.partial(lax.all_to_all, split_axis=0, concat_axis=0, tiled=True)
    up = [(i, i + 1) for i in range(frame_count - 1)]
    down = [(j, i) for i, j in up]

    def turned(parts):
        moved = [parts[0]]
        for d in range(1, peers):
            turn = [(i, (i + d) % peers) for i in range(peers)]
            moved.append(lax.ppermute(parts[d], "head", turn))
        return moved

    early, late = [0], list(range(1, HEADS_LOCAL))
    outgoing, near_on, tables = mask_tables(block_mask, frame_id, frame_count)
    lead = exchange(pack_lead(key_rows, value_rows, peers), "head")
    pair_parts, query_parts = pack_rest(me, queries, key_rows, value_rows, peers)
    parcel = select_blocks(outgoing, lead)
    far_early = exchange(parcel, "frame")
    flat = lead.reshape(FT, lead.shape[2])
    pairs = assemble(me, turned(pair_parts))
    parcel = select_blocks(outgoing, pairs)
    far_late = exchange(parcel, "frame")
    pairs = pairs.reshape(FT, pairs.shape[2])
    before_early = lax.ppermute(flat, "frame", up)
    after_early = lax.ppermute(flat, "frame", down)
    before_late = lax.ppermute(pairs, "frame", up)
    after_late = lax.ppermute(pairs, "frame", down)
    query = assemble(me, turned(query_parts))
    query = query.reshape(FT, query.shape[2])
    near_early = near_attention(near_on, query, early, flat, before_early, after_early)
    near_late = near_attention(near_on, query, late, pairs, before_late, after_late)
    early_out = far_attention(tables, me, query, early, far_early, near_early, peers)
    early_out = assemble(me, turned(early_out))
    (late_out,) = far_attention(tables, me, query, late, far_late, near_late, 1)
    late_out = exchange(late_out.reshape(peers, BLOCK, len(late) * HDIM), "head")
    return unpack(early_out, late_out)


def solution(mesh):
    placed = (
        P(("frame", "head"), None),
        P(("frame", "head"), None),
        P(("frame", "head"), None),
        P(),
    )
    return jax.shard_map(
        body, mesh=mesh, in_specs=placed, out_specs=P(("frame", "head"), None), check_vma=False
    )
```

```python
import functools
import math

import jax
import jax.numpy as jnp
from jax import lax
from jax.experimental import pallas as pl
from jax.experimental.pallas import tpu as pltpu
from jax.sharding import PartitionSpec as P

HDIM = 128
BLOCK = 128
BF = 8
FT = BF * BLOCK
HEADS_LOCAL = 3
GROUP = 4
SLAB = 4
TEAM = 4
PACK_STEPS = 4
LEAD_STEPS = 2
JOIN_STEPS = 2
PARAMS = pltpu.CompilerParams(vmem_limit_bytes=24 << 20)
NEG = -1e30
SCALE2 = math.log2(math.e) / math.sqrt(HDIM)
NT = (((1,), (1,)), ((), ()))
NN = (((1,), (0,)), ((), ()))


def in_hbm(*arrays):
    return [pltpu.with_memory_space_constraint(a, pltpu.HBM) for a in arrays]


def dot(a, b, dims):
    return lax.dot_general(a, b, dims, preferred_element_type=jnp.float32)


def lead_kernel(*refs):
    out_ref = refs[-1]
    group = out_ref.shape[0]
    for j in range(group):
        out_ref[j, :, :HDIM] = refs[j][...]
        out_ref[j, :, HDIM:] = refs[group + j][...]


def pack_lead(keys, values, peers):
    rows, width = keys.shape
    stride = width // peers // HDIM
    group = peers // LEAD_STEPS
    specs = [
        pl.BlockSpec((rows, HDIM), lambda i, j=j: (0, (i * group + j) * stride)) for j in range(group)
    ]
    keys, values = in_hbm(keys, values)
    return pl.pallas_call(
        lead_kernel,
        grid=(LEAD_STEPS,),
        in_specs=specs * 2,
        out_specs=pl.BlockSpec((group, rows, 2 * HDIM), lambda i: (i, 0, 0)),
        out_shape=pltpu.HBM((peers, rows, 2 * HDIM), keys.dtype),
        compiler_params=PARAMS,
        name="lead",
    )(*([keys] * group), *([values] * group))


def rest_kernel(me_ref, q_ref, k_ref, v_ref, *out_refs):
    peers = len(out_refs) // 2
    local = q_ref.shape[1] // peers
    heads = local // HDIM
    for d in range(peers):
        pair_ref, query_ref = out_refs[d], out_refs[peers + d]
        base = lax.rem(me_ref[0] + d, peers) * local
        for h in range(1, heads):
            cols = pl.ds(pl.multiple_of(base + h * HDIM, HDIM), HDIM)
            left = 2 * (h - 1) * HDIM
            pair_ref[:, left : left + HDIM] = k_ref[:, cols]
            pair_ref[:, left + HDIM : left + 2 * HDIM] = v_ref[:, cols]
        query_ref[...] = q_ref[:, pl.ds(pl.multiple_of(base, HDIM), local)]


def pack_rest(me, queries, keys, values, peers):
    rows, width = queries.shape
    local = width // peers
    tile = rows // PACK_STEPS
    spec = pl.BlockSpec((tile, width), lambda i, m: (i, 0))
    sizes = [2 * local - 2 * HDIM] * peers + [local] * peers
    outs = pl.pallas_call(
        rest_kernel,
        grid_spec=pltpu.PrefetchScalarGridSpec(
            num_scalar_prefetch=1,
            grid=(PACK_STEPS,),
            in_specs=[spec] * 3,
            out_specs=[pl.BlockSpec((tile, size), lambda i, m: (i, 0)) for size in sizes],
        ),
        out_shape=[pltpu.HBM((rows, size), queries.dtype) for size in sizes],
        compiler_params=PARAMS,
        name="rest",
    )(me, *in_hbm(queries, keys, values))
    return outs[:peers], outs[peers:]


def cross_kernel(me_ref, k_ref, v_ref, *out_refs):
    peers = len(out_refs)
    local = k_ref.shape[1] // peers
    for d, out_ref in enumerate(out_refs):
        base = lax.rem(me_ref[0] + d, peers) * local
        for h in range(local // HDIM):
            cols = pl.ds(pl.multiple_of(base + h * HDIM, HDIM), HDIM)
            left = 2 * h * HDIM
            out_ref[:, left : left + HDIM] = k_ref[:, cols]
            out_ref[:, left + HDIM : left + 2 * HDIM] = v_ref[:, cols]


def pack_cross(me, keys, values, peers):
    rows, width = keys.shape
    size = 2 * width // peers
    tile = rows // PACK_STEPS
    spec = pl.BlockSpec((tile, width), lambda i, m: (i, 0))
    return pl.pallas_call(
        cross_kernel,
        grid_spec=pltpu.PrefetchScalarGridSpec(
            num_scalar_prefetch=1,
            grid=(PACK_STEPS,),
            in_specs=[spec] * 2,
            out_specs=[pl.BlockSpec((tile, size), lambda i, m: (i, 0))] * peers,
        ),
        out_shape=[pltpu.HBM((rows, size), keys.dtype)] * peers,
        compiler_params=PARAMS,
        name="cross",
    )(me, *in_hbm(keys, values))


def gather_kernel(me_ref, *refs):
    out_ref = refs[-1]
    peers = len(refs) - 1
    for d, ref in enumerate(refs[:-1]):
        out_ref[lax.rem(me_ref[0] - d + peers, peers)] = ref[...]


def assemble(me, parts):
    peers = len(parts)
    rows, size = parts[0].shape
    tile = rows // JOIN_STEPS
    return pl.pallas_call(
        gather_kernel,
        grid_spec=pltpu.PrefetchScalarGridSpec(
            num_scalar_prefetch=1,
            grid=(JOIN_STEPS,),
            in_specs=[pl.BlockSpec((tile, size), lambda i, m: (i, 0))] * peers,
            out_specs=pl.BlockSpec((peers, tile, size), lambda i, m: (0, i, 0)),
        ),
        out_shape=pltpu.HBM((peers, rows, size), parts[0].dtype),
        compiler_params=PARAMS,
        name="assemble",
    )(me, *parts)


def unpack_kernel(early_ref, late_ref, out_ref, sem):
    peers = late_ref.shape[0]
    copies, left = [], 0
    for j in range(peers):
        for part, ref in enumerate((early_ref, late_ref)):
            cols = slice(left, left + ref.shape[2])
            left += ref.shape[2]
            copies.append(
                pltpu.make_async_copy(ref.at[j], out_ref.at[:, cols], sem.at[2 * j + part])
            )
    for copy in copies:
        copy.start()
    for copy in copies:
        copy.wait()


def unpack(early, late):
    peers, rows, width = late.shape
    return pl.pallas_call(
        unpack_kernel,
        in_specs=[pl.BlockSpec(memory_space=pltpu.VMEM)] * 2,
        out_specs=pl.BlockSpec(memory_space=pl.ANY),
        out_shape=pltpu.HBM((rows, peers * (early.shape[2] + width)), late.dtype),
        scratch_shapes=[pltpu.SemaphoreType.DMA((2 * peers,))],
        compiler_params=PARAMS,
        name="unpack",
    )(early, late)


def select_kernel(pick_ref, kv_ref, out_ref, sem):
    copies = [
        pltpu.make_async_copy(kv_ref.at[pick_ref[i]], out_ref.at[i], sem.at[i])
        for i in range(out_ref.shape[0])
    ]
    for copy in copies:
        copy.start()
    for copy in copies:
        copy.wait()


def select_blocks(picks, blocks):
    frames = picks.shape[0]
    _, rows, width = blocks.shape
    return pl.pallas_call(
        select_kernel,
        in_specs=[
            pl.BlockSpec(memory_space=pltpu.SMEM),
            pl.BlockSpec(memory_space=pltpu.VMEM),
        ],
        out_specs=pl.BlockSpec(memory_space=pl.ANY),
        out_shape=pltpu.HBM((frames, rows, width), blocks.dtype),
        scratch_shapes=[pltpu.SemaphoreType.DMA((frames,))],
        compiler_params=PARAMS,
        name="select",
    )(picks, blocks)


def near_kernel(on_ref, q_ref, own_ref, before_ref, after_ref, o_ref, m_ref, l_ref):
    tile = q_ref.shape[0]
    sub = tile // BLOCK
    first = pl.program_id(1) * sub
    query = q_ref[...]
    parts = [dot(query, own_ref[:, :HDIM], NT)]
    for side, ref in enumerate((before_ref, after_ref)):
        scores = dot(query, ref[:, :HDIM], NT)
        rows = []
        for s in range(sub):
            cols = []
            for b in range(BF):
                bias = jnp.where(on_ref[first + s, side * BF + b] > 0, 0.0, NEG)
                cols.append(
                    scores[s * BLOCK : (s + 1) * BLOCK, b * BLOCK : (b + 1) * BLOCK] + bias
                )
            rows.append(jnp.concatenate(cols, axis=1))
        parts.append(jnp.concatenate(rows, axis=0))
    top = functools.reduce(jnp.maximum, [jnp.max(p, axis=1, keepdims=True) for p in parts])
    mass = jnp.zeros((tile, HDIM), jnp.float32)
    summed = jnp.zeros((tile, HDIM), jnp.float32)
    for part, ref in zip(parts, (own_ref, before_ref, after_ref)):
        weights = jnp.exp2((part - top) * SCALE2)
        for b in range(BF):
            mass = mass + weights[:, b * BLOCK : (b + 1) * BLOCK]
        summed = summed + dot(weights.astype(jnp.bfloat16), ref[:, HDIM:], NN)
    o_ref[...] = summed
    m_ref[...] = jnp.broadcast_to(top, (tile, HDIM))
    l_ref[...] = mass


def near_attention(near_on, query, group, own, before, after):
    tile = 256
    rows = query.shape[0]
    heads = len(group)
    first = group[0]
    whole = pl.BlockSpec((rows, 2 * HDIM), lambda h, i, on: (0, h))
    return pl.pallas_call(
        near_kernel,
        grid_spec=pltpu.PrefetchScalarGridSpec(
            num_scalar_prefetch=1,
            grid=(heads, rows // tile),
            in_specs=[
                pl.BlockSpec((tile, HDIM), lambda h, i, on: (i, first + h)),
                whole,
                whole,
                whole,
            ],
            out_specs=[pl.BlockSpec((tile, HDIM), lambda h, i, on: (i, h))] * 3,
        ),
        out_shape=[pltpu.HBM((rows, heads * HDIM), jnp.float32)] * 3,
        cost_estimate=pl.CostEstimate(
            flops=12 * heads * rows * rows * HDIM,
            bytes_accessed=8 * heads * rows * 2 * HDIM,
            transcendentals=3 * heads * rows * rows,
        ),
        compiler_params=PARAMS,
        name="near",
    )(near_on, query, own, before, after)


def far_kernel(list_ref, rank_ref, count_ref, me_ref, q_ref, kv_ref, o_ref, m_ref, l_ref, *refs):
    out_refs, (m_s, l_s, acc_s) = refs[:-3], refs[-3:]
    m_s[...] = m_ref[...]
    l_s[...] = l_ref[...]
    acc_s[...] = o_ref[...]
    blocks = q_ref.shape[0] // BLOCK

    def step(lead, t, carry):
        units = []
        for s in range(lead, lead + TEAM):
            qb = rank_ref[s]
            rows = pl.ds(pl.multiple_of(qb * BLOCK, BLOCK), BLOCK)
            frames = [list_ref[qb, t * GROUP + i] for i in range(GROUP)]
            keys = jnp.concatenate([kv_ref[f, :, :HDIM] for f in frames], axis=0)
            raw = dot(q_ref[rows, :], keys, NT)
            units.append((qb, rows, frames, raw, m_s[rows, :], l_s[rows, :], acc_s[rows, :]))
        soft = []
        for qb, rows, frames, raw, old, mass, acc in units:
            scores = []
            for i in range(GROUP):
                bias = jnp.where(t * GROUP + i < count_ref[qb], 0.0, NEG)
                scores.append(raw[:, i * BLOCK : (i + 1) * BLOCK] + bias)
            peak = functools.reduce(jnp.maximum, scores)
            top = jnp.maximum(old, jnp.max(peak, axis=1, keepdims=True))
            fade = jnp.exp2((old - top) * SCALE2)
            weights = [jnp.exp2((s - top) * SCALE2) for s in scores]
            rounded = jnp.concatenate([w.astype(jnp.bfloat16) for w in weights], axis=1)
            mass = mass * fade + functools.reduce(jnp.add, weights)
            soft.append((rows, frames, top, mass, acc * fade, rounded))
        done = []
        for rows, frames, top, mass, acc, rounded in soft:
            values = jnp.concatenate([kv_ref[f, :, HDIM:] for f in frames], axis=0)
            done.append((rows, top, mass, acc + dot(rounded, values, NN)))
        for rows, top, mass, acc in done:
            m_s[rows, :] = top
            l_s[rows, :] = mass
            acc_s[rows, :] = acc
        return carry

    for lead in range(0, blocks, TEAM):
        trips = (count_ref[rank_ref[lead]] + GROUP - 1) // GROUP
        lax.fori_loop(0, trips, functools.partial(step, lead), 0)
    peers = len(out_refs)
    for d, out_ref in enumerate(out_refs):
        rows = slice(None)
        if peers > 1:
            block = lax.rem(me_ref[0] + d, peers)
            rows = pl.ds(pl.multiple_of(block * BLOCK, BLOCK), BLOCK)
        total = jnp.sum(l_s[rows, :], axis=1, keepdims=True)
        out_ref[...] = (acc_s[rows, :] / total).astype(out_ref.dtype)


def far_attention(tables, me, query, heads, far, near, pieces):
    rows = query.shape[0]
    first = heads[0]
    frames = far.shape[0]
    full = pl.BlockSpec((rows, HDIM), lambda g, a, b, c, m: (0, g))
    out = pl.BlockSpec((rows // pieces, HDIM), lambda g, a, b, c, m: (0, g))
    return pl.pallas_call(
        far_kernel,
        grid_spec=pltpu.PrefetchScalarGridSpec(
            num_scalar_prefetch=4,
            grid=(len(heads),),
            in_specs=[
                pl.BlockSpec((rows, HDIM), lambda g, a, b, c, m: (0, first + g)),
                pl.BlockSpec((frames, BLOCK, 2 * HDIM), lambda g, a, b, c, m: (0, 0, g)),
                full,
                full,
                full,
            ],
            out_specs=[out] * pieces,
            scratch_shapes=[
                pltpu.VMEM((rows, HDIM), jnp.float32),
                pltpu.VMEM((rows, HDIM), jnp.float32),
                pltpu.VMEM((rows, HDIM), jnp.float32),
            ],
        ),
        out_shape=[pltpu.HBM((rows // pieces, len(heads) * HDIM), query.dtype)] * pieces,
        cost_estimate=pl.CostEstimate(
            flops=len(heads) * rows * frames * BLOCK * HDIM,
            bytes_accessed=len(heads) * frames * BLOCK * 2 * HDIM * 2,
            transcendentals=len(heads) * rows * frames * BLOCK // 4,
        ),
        compiler_params=PARAMS,
        name="far",
    )(*tables, me, query, far, *in_hbm(*near))


def mask_tables(block_mask, frame_id, frame_count):
    block_ids = jnp.arange(BF, dtype=jnp.int32)
    frame_ids = jnp.arange(frame_count, dtype=jnp.int32)
    towards = lax.dynamic_slice_in_dim(block_mask, frame_id * BF, BF, 1)
    towards = jnp.max(towards.reshape(frame_count, BF, BF), axis=1)
    outgoing = jnp.minimum(jnp.sum(towards * block_ids[None, :], axis=1), BF - 1)
    own = lax.dynamic_slice_in_dim(block_mask, frame_id * BF, BF, 0)
    padded = jnp.pad(own, ((0, 0), (BF, BF)))
    beside = lax.dynamic_slice_in_dim(padded, frame_id * BF, 3 * BF, 1)
    near_on = jnp.concatenate([beside[:, :BF], beside[:, 2 * BF :]], axis=1)
    distant = (jnp.abs(frame_ids - frame_id) >= 2).astype(jnp.int32)
    active = jnp.max(own.reshape(BF, frame_count, BF), axis=2) * distant[None, :]
    upto = (frame_ids[:, None] <= frame_ids[None, :]).astype(jnp.int32)
    place = jnp.sum(active[:, :, None] * upto[None, :, :], axis=1)
    counts = jnp.sum(active, axis=1)
    slots = jnp.where(active > 0, place - 1, -1)
    hit = (slots[:, :, None] == frame_ids[None, None, :]).astype(jnp.int32)
    order = jnp.sum(hit * frame_ids[None, :, None], axis=1)
    ids = block_ids
    ahead = (counts[None, :] > counts[:, None]) | (
        (counts[None, :] == counts[:, None]) & (ids[None, :] < ids[:, None])
    )
    seat = jnp.sum(ahead.astype(jnp.int32), axis=1)
    rank = jnp.sum((seat[:, None] == ids[None, :]).astype(jnp.int32) * ids[:, None], axis=0)
    return outgoing, near_on, (order, rank, counts)


def body(queries, key_rows, value_rows, block_mask):
    frame_count = lax.axis_size("frame")
    peers = lax.axis_size("head")
    frame_id = lax.axis_index("frame")
    me = lax.axis_index("head").astype(jnp.int32).reshape(1)
    exchange = functools.partial(lax.all_to_all, split_axis=0, concat_axis=0, tiled=True)
    slabs = range(frame_count // SLAB)
    last = SLAB - 1
    up = [(i, i + 1) for i in range(frame_count - 1) if i % SLAB != last]
    down = [(j, i) for i, j in up]
    ahead = [(z * SLAB + last, (z + 1) * SLAB + last) for z in slabs[:-1]]
    behind = [(z * SLAB, (z - 1) * SLAB) for z in slabs[1:]]
    inward = [(z * SLAB + last, z * SLAB) for z in slabs[1:]]
    inward += [(z * SLAB, z * SLAB + last) for z in slabs[:-1]]

    def turned(parts):
        moved = [parts[0]]
        for d in range(1, peers):
            turn = [(i, (i + d) % peers) for i in range(peers)]
            moved.append(lax.ppermute(parts[d], "head", turn))
        return moved

    early, late = [0], list(range(1, HEADS_LOCAL))
    outgoing, near_on, tables = mask_tables(block_mask, frame_id, frame_count)
    lead = exchange(pack_lead(key_rows, value_rows, peers), "head")
    cross_keys = lax.ppermute(key_rows, "frame", ahead + behind)
    cross_values = lax.ppermute(value_rows, "frame", ahead + behind)
    pair_parts, query_parts = pack_rest(me, queries, key_rows, value_rows, peers)
    parcel = select_blocks(outgoing, lead)
    far_early = exchange(parcel, "frame")
    cross_parts = pack_cross(me, cross_keys, cross_values, peers)
    flat = lead.reshape(FT, lead.shape[2])
    pairs = assemble(me, turned(pair_parts))
    parcel = select_blocks(outgoing, pairs)
    far_late = exchange(parcel, "frame")
    pairs = pairs.reshape(FT, pairs.shape[2])
    before_early = lax.ppermute(flat, "frame", up)
    after_early = lax.ppermute(flat, "frame", down)
    before_late = lax.ppermute(pairs, "frame", up)
    after_late = lax.ppermute(pairs, "frame", down)
    folded = []
    for d in range(peers):
        pairs_of = [
            (i * peers + j, k * peers + (j + d) % peers) for i, k in inward for j in range(peers)
        ]
        folded.append(lax.ppermute(cross_parts[d], ("frame", "head"), pairs_of))
    cross = assemble(me, folded)
    cross = cross.reshape(FT, cross.shape[2])
    place = lax.rem(frame_id, SLAB)
    split = flat.shape[1]
    before_early = jnp.where(place == 0, cross[:, :split], before_early)
    before_late = jnp.where(place == 0, cross[:, split:], before_late)
    after_early = jnp.where(place == last, cross[:, :split], after_early)
    after_late = jnp.where(place == last, cross[:, split:], after_late)
    query = assemble(me, turned(query_parts))
    query = query.reshape(FT, query.shape[2])
    near_early = near_attention(near_on, query, early, flat, before_early, after_early)
    near_late = near_attention(near_on, query, late, pairs, before_late, after_late)
    early_out = far_attention(tables, me, query, early, far_early, near_early, peers)
    early_out = assemble(me, turned(early_out))
    (late_out,) = far_attention(tables, me, query, late, far_late, near_late, 1)
    late_out = exchange(late_out.reshape(peers, BLOCK, len(late) * HDIM), "head")
    return unpack(early_out, late_out)


def solution(mesh):
    placed = (
        P(("frame", "head"), None),
        P(("frame", "head"), None),
        P(("frame", "head"), None),
        P(),
    )
    return jax.shard_map(
        body, mesh=mesh, in_specs=placed, out_specs=P(("frame", "head"), None), check_vma=False
    )
```

```python
import functools
import math

import jax
import jax.numpy as jnp
from jax import lax
from jax.experimental import pallas as pl
from jax.experimental.pallas import tpu as pltpu
from jax.sharding import PartitionSpec as P

HDIM = 128
BLOCK = 128
BF = 8
FT = BF * BLOCK
HEADS_LOCAL = 3
GROUP = 4
TEAM = 4
PACK_STEPS = 4
LEAD_STEPS = 2
JOIN_STEPS = 2
PARAMS = pltpu.CompilerParams(vmem_limit_bytes=24 << 20)
NEG = -1e30
SCALE2 = math.log2(math.e) / math.sqrt(HDIM)
NT = (((1,), (1,)), ((), ()))
NN = (((1,), (0,)), ((), ()))


def in_hbm(*arrays):
    return [pltpu.with_memory_space_constraint(a, pltpu.HBM) for a in arrays]


def dot(a, b, dims):
    return lax.dot_general(a, b, dims, preferred_element_type=jnp.float32)


def lead_kernel(*refs):
    out_ref = refs[-1]
    group = out_ref.shape[0]
    for j in range(group):
        out_ref[j, :, :HDIM] = refs[j][...]
        out_ref[j, :, HDIM:] = refs[group + j][...]


def pack_lead(keys, values, peers):
    rows, width = keys.shape
    stride = width // peers // HDIM
    group = peers // LEAD_STEPS
    specs = [
        pl.BlockSpec((rows, HDIM), lambda i, j=j: (0, (i * group + j) * stride)) for j in range(group)
    ]
    keys, values = in_hbm(keys, values)
    return pl.pallas_call(
        lead_kernel,
        grid=(LEAD_STEPS,),
        in_specs=specs * 2,
        out_specs=pl.BlockSpec((group, rows, 2 * HDIM), lambda i: (i, 0, 0)),
        out_shape=pltpu.HBM((peers, rows, 2 * HDIM), keys.dtype),
        compiler_params=PARAMS,
        name="lead",
    )(*([keys] * group), *([values] * group))


def pairs_kernel(me_ref, k_ref, v_ref, *out_refs):
    peers = len(out_refs)
    local = k_ref.shape[1] // peers
    for d, out_ref in enumerate(out_refs):
        base = lax.rem(me_ref[0] + d, peers) * local
        for h in range(1, local // HDIM):
            cols = pl.ds(pl.multiple_of(base + h * HDIM, HDIM), HDIM)
            left = 2 * (h - 1) * HDIM
            out_ref[:, left : left + HDIM] = k_ref[:, cols]
            out_ref[:, left + HDIM : left + 2 * HDIM] = v_ref[:, cols]


def queries_kernel(me_ref, q_ref, *out_refs):
    peers = len(out_refs)
    local = q_ref.shape[1] // peers
    for d, out_ref in enumerate(out_refs):
        base = lax.rem(me_ref[0] + d, peers) * local
        out_ref[...] = q_ref[:, pl.ds(pl.multiple_of(base, HDIM), local)]


def pack_turned(kernel, me, arrays, size, peers):
    rows, width = arrays[0].shape
    tile = rows // PACK_STEPS
    return pl.pallas_call(
        kernel,
        grid_spec=pltpu.PrefetchScalarGridSpec(
            num_scalar_prefetch=1,
            grid=(PACK_STEPS,),
            in_specs=[pl.BlockSpec((tile, width), lambda i, m: (i, 0))] * len(arrays),
            out_specs=[pl.BlockSpec((tile, size), lambda i, m: (i, 0))] * peers,
        ),
        out_shape=[pltpu.HBM((rows, size), arrays[0].dtype)] * peers,
        compiler_params=PARAMS,
    )(me, *in_hbm(*arrays))


def gather_kernel(me_ref, *refs):
    out_ref = refs[-1]
    peers = len(refs) - 1
    for d, ref in enumerate(refs[:-1]):
        out_ref[lax.rem(me_ref[0] - d + peers, peers)] = ref[...]


def assemble(me, parts):
    peers = len(parts)
    rows, size = parts[0].shape
    tile = rows // JOIN_STEPS
    return pl.pallas_call(
        gather_kernel,
        grid_spec=pltpu.PrefetchScalarGridSpec(
            num_scalar_prefetch=1,
            grid=(JOIN_STEPS,),
            in_specs=[pl.BlockSpec((tile, size), lambda i, m: (i, 0))] * peers,
            out_specs=pl.BlockSpec((peers, tile, size), lambda i, m: (0, i, 0)),
        ),
        out_shape=pltpu.HBM((peers, rows, size), parts[0].dtype),
        compiler_params=PARAMS,
        name="assemble",
    )(me, *parts)


def unpack_kernel(early_ref, late_ref, out_ref, sem):
    peers = late_ref.shape[0]
    copies, left = [], 0
    for j in range(peers):
        for part, ref in enumerate((early_ref, late_ref)):
            cols = slice(left, left + ref.shape[2])
            left += ref.shape[2]
            copies.append(
                pltpu.make_async_copy(ref.at[j], out_ref.at[:, cols], sem.at[2 * j + part])
            )
    for copy in copies:
        copy.start()
    for copy in copies:
        copy.wait()


def unpack(early, late):
    peers, rows, width = late.shape
    return pl.pallas_call(
        unpack_kernel,
        in_specs=[pl.BlockSpec(memory_space=pltpu.VMEM)] * 2,
        out_specs=pl.BlockSpec(memory_space=pl.ANY),
        out_shape=pltpu.HBM((rows, peers * (early.shape[2] + width)), late.dtype),
        scratch_shapes=[pltpu.SemaphoreType.DMA((2 * peers,))],
        compiler_params=PARAMS,
        name="unpack",
    )(early, late)


def select_kernel(pick_ref, kv_ref, out_ref, sem):
    copies = [
        pltpu.make_async_copy(kv_ref.at[pick_ref[i]], out_ref.at[i], sem.at[i])
        for i in range(out_ref.shape[0])
    ]
    for copy in copies:
        copy.start()
    for copy in copies:
        copy.wait()


def select_blocks(picks, blocks):
    frames = picks.shape[0]
    _, rows, width = blocks.shape
    return pl.pallas_call(
        select_kernel,
        in_specs=[
            pl.BlockSpec(memory_space=pltpu.SMEM),
            pl.BlockSpec(memory_space=pltpu.VMEM),
        ],
        out_specs=pl.BlockSpec(memory_space=pl.ANY),
        out_shape=pltpu.HBM((frames, rows, width), blocks.dtype),
        scratch_shapes=[pltpu.SemaphoreType.DMA((frames,))],
        compiler_params=PARAMS,
        name="select",
    )(picks, blocks)


def near_kernel(on_ref, q_ref, own_ref, before_ref, after_ref, o_ref, m_ref, l_ref):
    tile = q_ref.shape[0]
    sub = tile // BLOCK
    first = pl.program_id(1) * sub
    query = q_ref[...]
    parts = [dot(query, own_ref[:, :HDIM], NT)]
    for side, ref in enumerate((before_ref, after_ref)):
        scores = dot(query, ref[:, :HDIM], NT)
        rows = []
        for s in range(sub):
            cols = []
            for b in range(BF):
                bias = jnp.where(on_ref[first + s, side * BF + b] > 0, 0.0, NEG)
                cols.append(
                    scores[s * BLOCK : (s + 1) * BLOCK, b * BLOCK : (b + 1) * BLOCK] + bias
                )
            rows.append(jnp.concatenate(cols, axis=1))
        parts.append(jnp.concatenate(rows, axis=0))
    top = functools.reduce(jnp.maximum, [jnp.max(p, axis=1, keepdims=True) for p in parts])
    mass = jnp.zeros((tile, HDIM), jnp.float32)
    summed = jnp.zeros((tile, HDIM), jnp.float32)
    for part, ref in zip(parts, (own_ref, before_ref, after_ref)):
        weights = jnp.exp2((part - top) * SCALE2)
        for b in range(BF):
            mass = mass + weights[:, b * BLOCK : (b + 1) * BLOCK]
        summed = summed + dot(weights.astype(jnp.bfloat16), ref[:, HDIM:], NN)
    o_ref[...] = summed
    m_ref[...] = jnp.broadcast_to(top, (tile, HDIM))
    l_ref[...] = mass


def near_attention(near_on, query, group, own, before, after):
    tile = 256
    rows = query.shape[0]
    heads = len(group)
    first = group[0]
    whole = pl.BlockSpec((rows, 2 * HDIM), lambda h, i, on: (0, h))
    return pl.pallas_call(
        near_kernel,
        grid_spec=pltpu.PrefetchScalarGridSpec(
            num_scalar_prefetch=1,
            grid=(heads, rows // tile),
            in_specs=[
                pl.BlockSpec((tile, HDIM), lambda h, i, on: (i, first + h)),
                whole,
                whole,
                whole,
            ],
            out_specs=[pl.BlockSpec((tile, HDIM), lambda h, i, on: (i, h))] * 3,
        ),
        out_shape=[pltpu.HBM((rows, heads * HDIM), jnp.float32)] * 3,
        cost_estimate=pl.CostEstimate(
            flops=12 * heads * rows * rows * HDIM,
            bytes_accessed=8 * heads * rows * 2 * HDIM,
            transcendentals=3 * heads * rows * rows,
        ),
        compiler_params=PARAMS,
        name="near",
    )(near_on, query, own, before, after)


def far_kernel(list_ref, rank_ref, count_ref, me_ref, q_ref, kv_ref, o_ref, m_ref, l_ref, *refs):
    out_refs, (m_s, l_s, acc_s) = refs[:-3], refs[-3:]
    m_s[...] = m_ref[...]
    l_s[...] = l_ref[...]
    acc_s[...] = o_ref[...]
    blocks = q_ref.shape[0] // BLOCK

    def step(lead, t, carry):
        units = []
        for s in range(lead, lead + TEAM):
            qb = rank_ref[s]
            rows = pl.ds(pl.multiple_of(qb * BLOCK, BLOCK), BLOCK)
            frames = [list_ref[qb, t * GROUP + i] for i in range(GROUP)]
            keys = jnp.concatenate([kv_ref[f, :, :HDIM] for f in frames], axis=0)
            raw = dot(q_ref[rows, :], keys, NT)
            units.append((qb, rows, frames, raw, m_s[rows, :], l_s[rows, :], acc_s[rows, :]))
        soft = []
        for qb, rows, frames, raw, old, mass, acc in units:
            scores = []
            for i in range(GROUP):
                bias = jnp.where(t * GROUP + i < count_ref[qb], 0.0, NEG)
                scores.append(raw[:, i * BLOCK : (i + 1) * BLOCK] + bias)
            peak = functools.reduce(jnp.maximum, scores)
            top = jnp.maximum(old, jnp.max(peak, axis=1, keepdims=True))
            fade = jnp.exp2((old - top) * SCALE2)
            weights = [jnp.exp2((s - top) * SCALE2) for s in scores]
            rounded = jnp.concatenate([w.astype(jnp.bfloat16) for w in weights], axis=1)
            mass = mass * fade + functools.reduce(jnp.add, weights)
            soft.append((rows, frames, top, mass, acc * fade, rounded))
        done = []
        for rows, frames, top, mass, acc, rounded in soft:
            values = jnp.concatenate([kv_ref[f, :, HDIM:] for f in frames], axis=0)
            done.append((rows, top, mass, acc + dot(rounded, values, NN)))
        for rows, top, mass, acc in done:
            m_s[rows, :] = top
            l_s[rows, :] = mass
            acc_s[rows, :] = acc
        return carry

    for lead in range(0, blocks, TEAM):
        trips = (count_ref[rank_ref[lead]] + GROUP - 1) // GROUP
        lax.fori_loop(0, trips, functools.partial(step, lead), 0)
    peers = len(out_refs)
    for d, out_ref in enumerate(out_refs):
        rows = slice(None)
        if peers > 1:
            block = lax.rem(me_ref[0] + d, peers)
            rows = pl.ds(pl.multiple_of(block * BLOCK, BLOCK), BLOCK)
        total = jnp.sum(l_s[rows, :], axis=1, keepdims=True)
        out_ref[...] = (acc_s[rows, :] / total).astype(out_ref.dtype)


def far_attention(tables, me, query, heads, far, near, pieces):
    rows = query.shape[0]
    first = heads[0]
    frames = far.shape[0]
    full = pl.BlockSpec((rows, HDIM), lambda g, a, b, c, m: (0, g))
    out = pl.BlockSpec((rows // pieces, HDIM), lambda g, a, b, c, m: (0, g))
    return pl.pallas_call(
        far_kernel,
        grid_spec=pltpu.PrefetchScalarGridSpec(
            num_scalar_prefetch=4,
            grid=(len(heads),),
            in_specs=[
                pl.BlockSpec((rows, HDIM), lambda g, a, b, c, m: (0, first + g)),
                pl.BlockSpec((frames, BLOCK, 2 * HDIM), lambda g, a, b, c, m: (0, 0, g)),
                full,
                full,
                full,
            ],
            out_specs=[out] * pieces,
            scratch_shapes=[
                pltpu.VMEM((rows, HDIM), jnp.float32),
                pltpu.VMEM((rows, HDIM), jnp.float32),
                pltpu.VMEM((rows, HDIM), jnp.float32),
            ],
        ),
        out_shape=[pltpu.HBM((rows // pieces, len(heads) * HDIM), query.dtype)] * pieces,
        cost_estimate=pl.CostEstimate(
            flops=len(heads) * rows * frames * BLOCK * HDIM,
            bytes_accessed=len(heads) * frames * BLOCK * 2 * HDIM * 2,
            transcendentals=len(heads) * rows * frames * BLOCK // 4,
        ),
        compiler_params=PARAMS,
        name="far",
    )(*tables, me, query, far, *in_hbm(*near))


def mask_tables(block_mask, frame_id, frame_count):
    block_ids = jnp.arange(BF, dtype=jnp.int32)
    frame_ids = jnp.arange(frame_count, dtype=jnp.int32)
    towards = lax.dynamic_slice_in_dim(block_mask, frame_id * BF, BF, 1)
    towards = jnp.max(towards.reshape(frame_count, BF, BF), axis=1)
    outgoing = jnp.minimum(jnp.sum(towards * block_ids[None, :], axis=1), BF - 1)
    own = lax.dynamic_slice_in_dim(block_mask, frame_id * BF, BF, 0)
    padded = jnp.pad(own, ((0, 0), (BF, BF)))
    beside = lax.dynamic_slice_in_dim(padded, frame_id * BF, 3 * BF, 1)
    near_on = jnp.concatenate([beside[:, :BF], beside[:, 2 * BF :]], axis=1)
    distant = (jnp.abs(frame_ids - frame_id) >= 2).astype(jnp.int32)
    active = jnp.max(own.reshape(BF, frame_count, BF), axis=2) * distant[None, :]
    upto = (frame_ids[:, None] <= frame_ids[None, :]).astype(jnp.int32)
    place = jnp.sum(active[:, :, None] * upto[None, :, :], axis=1)
    counts = jnp.sum(active, axis=1)
    slots = jnp.where(active > 0, place - 1, -1)
    hit = (slots[:, :, None] == frame_ids[None, None, :]).astype(jnp.int32)
    order = jnp.sum(hit * frame_ids[None, :, None], axis=1)
    ids = block_ids
    ahead = (counts[None, :] > counts[:, None]) | (
        (counts[None, :] == counts[:, None]) & (ids[None, :] < ids[:, None])
    )
    seat = jnp.sum(ahead.astype(jnp.int32), axis=1)
    rank = jnp.sum((seat[:, None] == ids[None, :]).astype(jnp.int32) * ids[:, None], axis=0)
    return outgoing, near_on, (order, rank, counts)


def body(queries, key_rows, value_rows, block_mask):
    frame_count = lax.axis_size("frame")
    peers = lax.axis_size("head")
    frame_id = lax.axis_index("frame")
    me = lax.axis_index("head").astype(jnp.int32).reshape(1)
    exchange = functools.partial(lax.all_to_all, split_axis=0, concat_axis=0, tiled=True)
    up = [(i, i + 1) for i in range(frame_count - 1)]
    down = [(j, i) for i, j in up]

    def turned(parts):
        moved = [parts[0]]
        for d in range(1, peers):
            turn = [(i, (i + d) % peers) for i in range(peers)]
            moved.append(lax.ppermute(parts[d], "head", turn))
        return moved

    early, late = [0], list(range(1, HEADS_LOCAL))
    outgoing, near_on, tables = mask_tables(block_mask, frame_id, frame_count)
    lead = exchange(pack_lead(key_rows, value_rows, peers), "head")
    local = queries.shape[1] // peers
    pair_parts = pack_turned(pairs_kernel, me, (key_rows, value_rows), 2 * local - 2 * HDIM, peers)
    query_parts = pack_turned(queries_kernel, me, (queries,), local, peers)
    parcel = select_blocks(outgoing, lead)
    far_early = exchange(parcel, "frame")
    flat = lead.reshape(FT, lead.shape[2])
    pairs = assemble(me, turned(pair_parts))
    parcel = select_blocks(outgoing, pairs)
    far_late = exchange(parcel, "frame")
    pairs = pairs.reshape(FT, pairs.shape[2])
    before_early = lax.ppermute(flat, "frame", up)
    after_early = lax.ppermute(flat, "frame", down)
    before_late = lax.ppermute(pairs, "frame", up)
    after_late = lax.ppermute(pairs, "frame", down)
    query = assemble(me, turned(query_parts))
    query = query.reshape(FT, query.shape[2])
    near_early = near_attention(near_on, query, early, flat, before_early, after_early)
    near_late = near_attention(near_on, query, late, pairs, before_late, after_late)
    early_out = far_attention(tables, me, query, early, far_early, near_early, peers)
    early_out = assemble(me, turned(early_out))
    (late_out,) = far_attention(tables, me, query, late, far_late, near_late, 1)
    late_out = exchange(late_out.reshape(peers, BLOCK, len(late) * HDIM), "head")
    return unpack(early_out, late_out)


def solution(mesh):
    placed = (
        P(("frame", "head"), None),
        P(("frame", "head"), None),
        P(("frame", "head"), None),
        P(),
    )
    return jax.shard_map(
        body, mesh=mesh, in_specs=placed, out_specs=P(("frame", "head"), None), check_vma=False
    )
```
